512 devices in a mesh: region: 16 (over y, z_hi, core), tile: 32 (over z_lo, x).
Axes of the slice: x: 4, y: 4, z: 16 (z_hi: 2, z_lo: 8; z = z_hi * 8 + z_lo), core: 2. Of those that a mesh axis runs over, the one named last changes fastest.
Arguments:
- image: bfloat16 [4, 4096, 8192], P(None, 'region', 'tile'), may hold values from -6 to 6
- amplitude: float32 [16, 32, 4, 12, 128], P('region', 'tile'), may hold values from -6 to 6
- positions: int32 [2, 16, 32, 128], P(None, 'region', 'tile'), may hold values from 0 to 255, as said below
- live: int32 [16, 32], P('region', 'tile'), may hold values from 32 to 128, as said below
- psf_rows: bfloat16 [4, 12, 31], replicated, may hold values from -2.5 to 2.5
- psf_cols: bfloat16 [4, 12, 31], replicated, may hold values from -2.5 to 2.5
Outputs:
- updated: float32 [16, 32, 4, 12, 128], P('region', 'tile')
- residual: float32 [4, 4096, 8192], P(None, 'region', 'tile')
The draws below stay inside these ranges and needn't reach their ends.
Inputs may be any that keep to these rules, and one draw needn't show every extreme that they name: `positions`: every centre lies inside its tile. A source's core reaches past the top edge exactly when its row is below 15, past the bottom edge exactly when its row is above 240, and likewise for columns with 256. The slots of block q = s // 4, for q below 8, hold sources that reach past exactly the edges of direction q, in the order top-left, top, top-right, left, right, bottom-left, bottom, bottom-right; every slot from 32 on holds a source that reaches past no edge. `live`: some tile uses all 128 slots.
All inputs are finite; a program needn't handle non-finite values.
Results may differ from the reference program's by a relative error of at most 0.0011.
Values may be sent and summed in bfloat16 or wider, within the bound.
No kernel may reach another device: no remote copies, remote signals or barrier semaphores. Data moves between devices by JAX's collectives and lax.ppermute only.
A program may use at most 64 MiB of HBM per device.

```python
import jax
import jax.numpy as jnp
from jax import lax

B = 4
K = 12
TAPS = 31
RIM = 15
H = 256
W = 256
S = 128
CB = 4
REGIONS = 16
TILES = 32


def draw_live(key, part):
    key_level, key_chosen = jax.random.split(key)
    levels = jax.random.randint(key_level, (REGIONS, TILES), 0, 17)
    floor_count = 8 * CB
    counts = floor_count + (S - floor_count) * levels * levels // 256
    chosen = jax.random.randint(key_chosen, (), 0, REGIONS * TILES)
    flattened = jnp.where(jnp.arange(REGIONS * TILES) == chosen, S, counts.reshape(-1))
    return flattened.reshape(REGIONS, TILES).astype(jnp.int32)


def draw_positions(key, part):
    key_rows, key_cols = jax.random.split(key)
    slot_index = jnp.arange(S, dtype=jnp.int32)
    block_index = jnp.minimum(slot_index // CB, 7)
    crossing = slot_index < 8 * CB
    row_table = jnp.array([0, 0, 0, 1, 1, 2, 2, 2], jnp.int32)
    col_table = jnp.array([0, 1, 2, 0, 2, 0, 1, 2], jnp.int32)
    row_side = jnp.where(crossing, row_table[block_index], 1)
    col_side = jnp.where(crossing, col_table[block_index], 1)
    row_lower = jnp.where(row_side == 0, 0, jnp.where(row_side == 1, RIM, H - RIM))
    row_upper = jnp.where(row_side == 0, RIM, jnp.where(row_side == 1, H - RIM, H))
    col_lower = jnp.where(col_side == 0, 0, jnp.where(col_side == 1, RIM, W - RIM))
    col_upper = jnp.where(col_side == 0, RIM, jnp.where(col_side == 1, W - RIM, W))
    shape_all = (REGIONS, TILES, S)
    rows_drawn = jax.random.randint(key_rows, shape_all, jnp.broadcast_to(row_lower, shape_all), jnp.broadcast_to(row_upper, shape_all))
    cols_drawn = jax.random.randint(key_cols, shape_all, jnp.broadcast_to(col_lower, shape_all), jnp.broadcast_to(col_upper, shape_all))
    return jnp.stack([rows_drawn, cols_drawn]).astype(jnp.int32)


def block_levels(rng, shape, cuts, low, high):
    def one(axis_at, parts):
        heights = jax.random.uniform(jax.random.fold_in(jax.random.fold_in(rng, 6), axis_at), (parts,), jnp.float32, low / len(cuts), high / len(cuts))
        return jnp.repeat(jnp.exp(heights), shape[axis_at] // parts).reshape((-1,) + (1,) * (len(shape) - axis_at - 1))

    level = one(*cuts[0])
    for cut in cuts[1:]:
        level = level * one(*cut)
    return level


def centred(rng, extent, deviation, reach, cuts=(), held_as=jnp.bfloat16):
    level = block_levels(rng, extent, cuts, -0.22, 0.18) if cuts else 1.0
    values = jax.random.normal(rng, extent, jnp.float32) * deviation * level
    return jnp.minimum(jnp.maximum(values, -reach), reach).astype(held_as)


def setup_inputs(seed: int = 0) -> dict:
    keys = jax.random.split(jax.random.key(seed), 7)
    image = centred(keys[0], (B, REGIONS * H, TILES * W), 1.0, 6.0, ((1, 16), (2, 32)))
    amplitude = centred(keys[1], (REGIONS, TILES, B, K, S), 1.0, 6.0, ((0, 16), (1, 32)), jnp.float32)
    positions = draw_positions(jax.random.fold_in(keys[6], 71), 0)
    live = draw_live(jax.random.fold_in(keys[6], 71), 0)
    psf_rows = centred(keys[4], (B, K, TAPS), 0.3, 2.5)
    psf_cols = centred(keys[5], (B, K, TAPS), 0.3, 2.5)
    return dict(image=image, amplitude=amplitude, positions=positions, live=live, psf_rows=psf_rows, psf_cols=psf_cols)


step_rate = 0.05


def reference(image, amplitude, positions, live, psf_rows, psf_cols):
    rows_real = psf_rows.astype(jnp.float32)
    cols_real = psf_cols.astype(jnp.float32)
    tap_range = jnp.arange(TAPS, dtype=jnp.int32)
    slot_range = jnp.arange(S, dtype=jnp.int32)

    def tile_setup(tile_number):
        region_index = (tile_number // TILES).astype(jnp.int32)
        tile_index = (tile_number % TILES).astype(jnp.int32)
        fluxes = amplitude[region_index, tile_index]
        alive_mask = (slot_range < live[region_index, tile_index]).astype(jnp.float32)
        row_start = region_index * H + positions[0, region_index, tile_index]
        col_start = tile_index * W + positions[1, region_index, tile_index]
        rows_at = (row_start[:, None] + tap_range[None, :]).astype(jnp.int32)
        cols_at = (col_start[:, None] + tap_range[None, :]).astype(jnp.int32)
        return fluxes, alive_mask, rows_at, cols_at

    def add_tile(tile_number, canvas):
        fluxes, alive_mask, rows_at, cols_at = tile_setup(tile_number)
        masked = fluxes * alive_mask
        scaled = (masked[:, :, :, None] * rows_real[:, :, None, :]).astype(jnp.bfloat16)
        scaled = lax.optimization_barrier(scaled).astype(jnp.float32)
        cores = jnp.einsum("bksi,bkj->bsij", scaled, cols_real)
        return canvas.at[:, rows_at[:, :, None], cols_at[:, None, :]].add(cores)

    canvas = jnp.zeros((B, REGIONS * H + 2 * RIM, TILES * W + 2 * RIM), jnp.float32)
    canvas = lax.fori_loop(0, REGIONS * TILES, add_tile, canvas)
    model = canvas[:, RIM:RIM + REGIONS * H, RIM:RIM + TILES * W]
    residual = image.astype(jnp.float32) - model
    rounded = lax.optimization_barrier(residual.astype(jnp.bfloat16))
    padded = jnp.pad(rounded.astype(jnp.float32), ((0, 0), (RIM, RIM), (RIM, RIM)))

    def tile_update(tile_number):
        fluxes, alive_mask, rows_at, cols_at = tile_setup(tile_number)
        window = padded[:, rows_at[:, :, None], cols_at[:, None, :]]
        inner = jnp.einsum("bsij,bkj->bksi", window, cols_real)
        gradient = jnp.einsum("bksi,bki->bks", inner, rows_real)
        return fluxes + step_rate * gradient * alive_mask

    numbers = jnp.arange(REGIONS * TILES, dtype=jnp.int32)
    updated = lax.map(tile_update, numbers).reshape(REGIONS, TILES, B, K, S)
    return updated, residual
```

```python
import functools

import jax
import jax.numpy as jnp
from jax import lax
from jax.experimental import pallas as pl
from jax.experimental.pallas import tpu as pltpu
from jax.sharding import PartitionSpec as P

step_rate = 0.05
PAD = 16
LANES = 128
CROSS = 32
NT = (((1,), (1,)), ((), ()))
NN = (((1,), (0,)), ((), ()))


def lookup(row, index):
    return jnp.take_along_axis(jnp.broadcast_to(row, index.shape), index, axis=1)


def grouped(value):
    rows = lax.broadcasted_iota(jnp.int32, value.shape, 0)
    total = jnp.where(rows % 4 == 0, value, 0.0)
    for i in range(1, 4):
        total = total + jnp.where(rows % 4 == i, pltpu.roll(value, CROSS * i, axis=1), 0.0)
    return [jnp.sum(total[4 * j : 4 * j + 4], axis=0, keepdims=True) for j in range(3)]


def tap_index(pixel, centre, taps, outside, base=0):
    tap = pixel - centre + (taps - 1) // 2
    return jnp.where((tap >= 0) & (tap < taps), tap, outside) + base


def render_kernel(
    scalars, pos, amp, psf_rows, psf_cols, image,
    field, side, send_a, send_b, table_y, table_x, cross_y, cross_x,
    tmpl_y, tmpl_x, flux, index_y, index_x, scaled, cross_scaled,
):
    bands, comps, taps = psf_rows.shape
    height, width = image.shape[1], image.shape[2]
    ext = height + 2 * PAD
    even = scalars[0] == 0
    live = scalars[2]
    lane = lax.broadcasted_iota(jnp.int32, (1, LANES), 1)
    tmpl_y[...] = jnp.zeros_like(tmpl_y)
    tmpl_x[...] = jnp.zeros_like(tmpl_x)
    tmpl_y[:, :, :taps] = psf_rows[...].astype(jnp.float32)
    tmpl_x[:, :, :taps] = psf_cols[...].astype(jnp.float32)
    flux[...] = jnp.where(lane < live, amp[...], 0.0)
    row, col = pos[0:1, :], pos[1:2, :]
    pixel_y = lax.broadcasted_iota(jnp.int32, (ext, LANES), 0) - PAD
    index_y[...] = tap_index(pixel_y, row, taps, LANES - 1)
    pixel_x = lax.broadcasted_iota(jnp.int32, (width, LANES), 0)
    index_x[...] = tap_index(pixel_x, col, taps, LANES - 1)

    def one_band(b, carry):
        for k in range(comps):
            cut = pl.ds(k * LANES, LANES)
            placed = lookup(tmpl_y[b, k : k + 1, :], index_y[...])
            table_y[b, :, cut] = placed.astype(jnp.bfloat16)
            scaled[:, cut] = (placed * flux[b, k : k + 1, :]).astype(jnp.bfloat16)
            table_x[b, :, cut] = lookup(tmpl_x[b, k : k + 1, :], index_x[...]).astype(jnp.bfloat16)
        model = lax.dot_general(scaled[...], table_x[b], NT, preferred_element_type=jnp.float32)
        field[b] = -model
        field[b, pl.ds(PAD, height), :] += image[b].astype(jnp.float32)
        return carry

    lax.fori_loop(0, bands, one_band, 0)

    first = jnp.where(lane < CROSS, row, 0)
    second = jnp.where(lane < CROSS, col, 0)
    row_four = first
    col_four = second
    for i in range(1, 4):
        row_four = row_four + pltpu.roll(first, CROSS * i, axis=1)
        col_four = col_four + pltpu.roll(second, CROSS * i, axis=1)
    base = (lane // CROSS) * CROSS
    cross_index_y = tap_index(pixel_y, row_four, taps, CROSS - 1, base)
    outer = lax.broadcasted_iota(jnp.int32, (CROSS, LANES), 0)
    outer = jnp.where(outer < PAD, outer - PAD, outer + width - PAD)
    cross_index_x = tap_index(outer, col_four, taps, CROSS - 1, base)
    cross_x[...] = jnp.zeros_like(cross_x)
    for b in range(bands):
        four_y = grouped(tmpl_y[b])
        four_x = grouped(tmpl_x[b])
        four_flux = grouped(jnp.where(lane < CROSS, flux[b], 0.0))
        for j in range(comps // 4):
            cut = pl.ds((b * (comps // 4) + j) * LANES, LANES)
            placed = lookup(four_y[j], cross_index_y)
            cross_y[:, cut] = placed.astype(jnp.bfloat16)
            cross_scaled[:, cut] = (placed * four_flux[j]).astype(jnp.bfloat16)
            cross_x[pl.ds(b * CROSS, CROSS), cut] = lookup(four_x[j], cross_index_x).astype(jnp.bfloat16)
    side[...] = -lax.dot_general(cross_scaled[...], cross_x[...], NT, preferred_element_type=jnp.float32)

    start_a = pl.multiple_of(jnp.where(even, height, 0), 2 * PAD)
    start_b = pl.multiple_of(jnp.where(even, 0, height), 2 * PAD)
    for send, start in ((send_a, start_a), (send_b, start_b)):
        for b in range(bands):
            send[pl.ds(b * 2 * PAD, 2 * PAD), :] = field[b, pl.ds(start, 2 * PAD), :].astype(jnp.bfloat16)
        wide = side[pl.ds(start, 2 * PAD), :].astype(jnp.bfloat16)
        send[pl.ds(bands * 2 * PAD, PAD), pl.ds(0, LANES)] = wide[:PAD]
        send[pl.ds(bands * 2 * PAD, PAD), pl.ds(LANES, LANES)] = wide[PAD:]


def add_rows(scalars, field, side, got_a, got_b):
    bands, ext = field.shape[0], field.shape[1]
    height = ext - 2 * PAD
    even = scalars[0] == 0
    start_a = pl.multiple_of(jnp.where(even, height, 0), 2 * PAD)
    start_b = pl.multiple_of(jnp.where(even, 0, height), 2 * PAD)
    for got, start in ((got_a, start_a), (got_b, start_b)):
        for b in range(bands):
            field[b, pl.ds(start, 2 * PAD), :] += got[pl.ds(b * 2 * PAD, 2 * PAD), :].astype(jnp.float32)
        side[pl.ds(start, PAD), :] += got[pl.ds(bands * 2 * PAD, PAD), pl.ds(0, LANES)].astype(jnp.float32)
        side[pl.ds(start + PAD, PAD), :] += got[pl.ds(bands * 2 * PAD, PAD), pl.ds(LANES, LANES)].astype(jnp.float32)


def column_kernel(scalars, field_in, side_in, got_a, got_b, field, side, send_a, send_b):
    bands, ext, width = field.shape
    field[...] = field_in[...]
    side[...] = side_in[...]
    add_rows(scalars, field, side, got_a, got_b)
    even = scalars[1] == 0
    lane = lax.broadcasted_iota(jnp.int32, (1, LANES), 1)
    to_left = side[...]
    to_right = side[...]
    for b in range(bands):
        low = pltpu.roll(field[b, :, pl.ds(0, LANES)], CROSS * b + PAD, axis=1)
        to_left = jnp.where((lane >= CROSS * b + PAD) & (lane < CROSS * (b + 1)), low, to_left)
        high = pltpu.roll(field[b, :, pl.ds(width - LANES, LANES)], CROSS * b + PAD, axis=1)
        to_right = jnp.where((lane >= CROSS * b) & (lane < CROSS * b + PAD), high, to_right)
    send_a[...] = jnp.where(even, to_right, to_left).astype(jnp.bfloat16)
    send_b[...] = jnp.where(even, to_left, to_right).astype(jnp.bfloat16)


def gradient_kernel(
    scalars, amp, field, side, got_a, got_b, table_y, table_x, cross_y, cross_x,
    updated, residual, total, gradient,
):
    bands, ext, width = field.shape
    height = ext - 2 * PAD
    comps = amp.shape[1]
    even = scalars[1] == 0
    live = scalars[2]
    lane = lax.broadcasted_iota(jnp.int32, (1, LANES), 1)
    from_a, from_b = got_a[...].astype(jnp.float32), got_b[...].astype(jnp.float32)
    from_left = jnp.where(even, from_b, from_a)
    from_right = jnp.where(even, from_a, from_b)
    total[...] = field[...]
    for b in range(bands):
        low = pltpu.roll(from_left, LANES - CROSS * b - PAD, axis=1)
        total[b, :, pl.ds(0, LANES)] += jnp.where(lane < PAD, low, 0.0)
        high = pltpu.roll(from_right, LANES - CROSS * b - PAD, axis=1)
        total[b, :, pl.ds(width - LANES, LANES)] += jnp.where(lane >= LANES - PAD, high, 0.0)
    outer = side[...] + jnp.where(lane % CROSS < PAD, from_left, from_right)
    low_row, high_row, low_col, high_col = scalars[3], scalars[4], scalars[5], scalars[6]
    pixel_y = lax.broadcasted_iota(jnp.int32, (ext, LANES), 0)
    inside = (pixel_y >= low_row) & (pixel_y < high_row)
    inside = inside & (lane % CROSS >= low_col) & (lane % CROSS < high_col)
    outer = jnp.where(inside, outer, 0.0)

    @pl.when(low_row > 0)
    def _():
        total[:, pl.ds(0, PAD), :] = jnp.zeros((bands, PAD, width), jnp.float32)

    @pl.when(high_row < ext)
    def _():
        total[:, pl.ds(ext - PAD, PAD), :] = jnp.zeros((bands, PAD, width), jnp.float32)

    for b in range(bands):
        residual[b] = total[b, pl.ds(PAD, height), :]

    def one_band(b, carry):
        rounded = total[b].astype(jnp.bfloat16)
        for k in range(0, comps, 2):
            cut = pl.ds(k * LANES, 2 * LANES)
            inner = lax.dot_general(rounded, table_x[b, :, cut], NN, preferred_element_type=jnp.float32)
            summed = jnp.sum(inner * table_y[b, :, cut].astype(jnp.float32), axis=0, keepdims=True)
            gradient[b, k : k + 1, :] = summed[:, :LANES]
            gradient[b, k + 1 : k + 2, :] = summed[:, LANES:]
        return carry

    lax.fori_loop(0, bands, one_band, 0)

    inner = lax.dot_general(outer.astype(jnp.bfloat16), cross_x[...], NN, preferred_element_type=jnp.float32)
    summed = jnp.sum(inner * cross_y[...].astype(jnp.float32), axis=0, keepdims=True)
    for b in range(bands):
        for j in range(comps // 4):
            start = (b * (comps // 4) + j) * LANES
            four = summed[:, start : start + LANES]
            for i in range(4):
                part = four if i == 0 else pltpu.roll(four, LANES - CROSS * i, axis=1)
                gradient[b, 4 * j + i : 4 * j + i + 1, :] += jnp.where(lane < CROSS, part, 0.0)
    updated[...] = amp[...] + step_rate * jnp.where(lane < live, gradient[...], 0.0)


SMEM = pl.BlockSpec(memory_space=pltpu.SMEM)
VMEM = pl.BlockSpec(memory_space=pltpu.VMEM)
params = pltpu.CompilerParams(vmem_limit_bytes=48 << 20)


def swaps(axis, first):
    out = []
    for i in range(first, lax.axis_size(axis) - 1, 2):
        out += [(i, i + 1), (i + 1, i)]
    return out


def on_device(image, amplitude, positions, live, psf_rows, psf_cols):
    amp = amplitude[0, 0]
    bands, height, width = image.shape
    comps, slots = amp.shape[1], amp.shape[2]
    ext = height + 2 * PAD
    shape = jax.ShapeDtypeStruct
    f32, bf16 = jnp.float32, jnp.bfloat16
    region, tile = lax.axis_index("region"), lax.axis_index("tile")
    scalars = jnp.stack([
        region % 2,
        tile % 2,
        live[0, 0],
        jnp.where(region == 0, PAD, 0),
        jnp.where(region == lax.axis_size("region") - 1, ext - PAD, ext),
        jnp.where(tile == 0, PAD, 0),
        jnp.where(tile == lax.axis_size("tile") - 1, PAD, 2 * PAD),
    ]).astype(jnp.int32)
    rows_sent = bands * 2 * PAD + PAD
    table_width = comps * slots
    field, side, send_a, send_b, table_y, table_x, cross_y, cross_x = pl.pallas_call(
        render_kernel,
        out_shape=[
            shape((bands, ext, width), f32), shape((ext, LANES), f32),
            shape((rows_sent, width), bf16), shape((rows_sent, width), bf16),
            shape((bands, ext, table_width), bf16), shape((bands, width, table_width), bf16),
            shape((ext, bands * comps * CROSS), bf16), shape((bands * CROSS, bands * comps * CROSS), bf16),
        ],
        in_specs=[SMEM] + [VMEM] * 5,
        out_specs=[VMEM] * 8,
        scratch_shapes=[
            pltpu.VMEM((bands, comps, LANES), f32), pltpu.VMEM((bands, comps, LANES), f32),
            pltpu.VMEM((bands, comps, LANES), f32),
            pltpu.VMEM((ext, LANES), jnp.int32), pltpu.VMEM((width, LANES), jnp.int32),
            pltpu.VMEM((ext, table_width), bf16), pltpu.VMEM((ext, bands * comps * CROSS), bf16),
        ],
        compiler_params=params,
    )(scalars, positions[:, 0, 0], amp, psf_rows, psf_cols, image)
    got_b = lax.ppermute(send_b, "region", swaps("region", 1))
    got_a = lax.ppermute(send_a, "region", swaps("region", 0))
    field, side, send_a, send_b = pl.pallas_call(
        column_kernel,
        out_shape=[
            shape((bands, ext, width), f32), shape((ext, LANES), f32),
            shape((ext, LANES), bf16), shape((ext, LANES), bf16),
        ],
        in_specs=[SMEM] + [VMEM] * 4,
        out_specs=[VMEM] * 4,
        compiler_params=params,
    )(scalars, field, side, got_a, got_b)
    got_b = lax.ppermute(send_b, "tile", swaps("tile", 1))
    got_a = lax.ppermute(send_a, "tile", swaps("tile", 0))
    updated, residual = pl.pallas_call(
        gradient_kernel,
        out_shape=[shape(amp.shape, f32), shape(image.shape, f32)],
        in_specs=[SMEM] + [VMEM] * 9,
        out_specs=[VMEM] * 2,
        scratch_shapes=[
            pltpu.VMEM((bands, ext, width), f32), pltpu.VMEM((bands, comps, LANES), f32),
        ],
        compiler_params=params,
    )(scalars, amp, field, side, got_a, got_b, table_y, table_x, cross_y, cross_x)
    return (updated[None, None], residual)


def solution(mesh):
    in_specs = (
        P(None, "region", "tile"),
        P("region", "tile", None, None, None),
        P(None, "region", "tile", None),
        P("region", "tile"),
        P(),
        P(),
    )
    out_specs = (P("region", "tile", None, None, None), P(None, "region", "tile"))
    return jax.shard_map(
        on_device, mesh=mesh, in_specs=in_specs, out_specs=out_specs, check_vma=False
    )
```

```python
import jax
import jax.numpy as jnp
from jax import lax
from jax.experimental import pallas as pl
from jax.experimental.pallas import tpu as pltpu
from jax.sharding import PartitionSpec as P

step_rate = 0.05
PAD = 16
LANES = 128
CROSS = 32
NT = (((1,), (1,)), ((), ()))
NN = (((1,), (0,)), ((), ()))


def lookup(row, index):
    return jnp.take_along_axis(jnp.broadcast_to(row, index.shape), index, axis=1)


def grouped(value):
    out = []
    for j in range(value.shape[0] // 4):
        total = value[4 * j]
        for i in range(1, 4):
            total = total + pltpu.roll(value[4 * j + i], CROSS * i, axis=1)
        out.append(total)
    return out


def place(dst, src, first, count, tile_of, offset, lanes):
    for i in range(count):
        here = [tile_of == first + i - j for j in range(3)]
        for k in range(lanes // LANES):
            cut = pl.ds(k * LANES, LANES)
            value = jnp.zeros((PAD, LANES), jnp.bfloat16)
            for j in range(3):
                value = jnp.where(here[j], src[pl.ds(PAD * j, PAD), cut], value)
            dst[pl.ds(offset + PAD * i, PAD), cut] = value


def tiles_of(centre):
    return jnp.broadcast_to((centre + 1) // PAD, (PAD, LANES)).astype(jnp.bfloat16)


def spread(value, lane):
    first = jnp.where(lane < CROSS, value, 0)
    out = first
    for i in range(1, 4):
        out = out + pltpu.roll(first, CROSS * i, axis=1)
    return out


def starts(scalars, height):
    even = scalars[0] == 0
    start_a = pl.multiple_of(jnp.where(even, height, 0), 2 * PAD)
    start_b = pl.multiple_of(jnp.where(even, 0, height), 2 * PAD)
    return start_a, start_b


def strip_kernel(
    scalars, pos_hbm, amp_hbm, psf_rows_hbm, psf_cols_hbm, image_hbm,
    send, fine_y, fine_scaled, table_x, cross_fine_y, cross_fine_scaled, cross_x,
    pos, amp, psf_rows, psf_cols, image, sems, tmpl_y, tmpl_x, flux, fine_x, strip, cross_strip, cross_fine_x,
):
    comps, bands, taps = psf_rows.shape
    width = table_x.shape[1]
    height = width
    start_b = starts(scalars, height)[1]
    top = scalars[0] == 0
    image_row = pl.multiple_of(jnp.where(top, 0, height - PAD), PAD)
    copies = [
        pltpu.make_async_copy(pos_hbm, pos, sems.at[0]),
        pltpu.make_async_copy(psf_cols_hbm, psf_cols, sems.at[1]),
        pltpu.make_async_copy(psf_rows_hbm, psf_rows, sems.at[2]),
        pltpu.make_async_copy(amp_hbm, amp, sems.at[3]),
        pltpu.make_async_copy(image_hbm.at[:, pl.ds(image_row, PAD), :], image, sems.at[4]),
    ]
    for copy in copies:
        copy.start()
    live = scalars[2]
    lane = lax.broadcasted_iota(jnp.int32, (1, LANES), 1)
    base = (lane // CROSS) * CROSS
    tmpl_y[...] = jnp.zeros_like(tmpl_y)
    tmpl_x[...] = jnp.zeros_like(tmpl_x)
    cross_x[...] = jnp.zeros_like(cross_x)
    for copy in copies[:4]:
        copy.wait()
    tmpl_y[:, :, :taps] = psf_rows[...].astype(jnp.float32)
    tmpl_x[:, :, :taps] = psf_cols[...].astype(jnp.float32)
    flux[...] = jnp.where(lane < live, amp[...], 0.0)
    row, col = pos[0:1, :], pos[1:2, :]
    inner = lax.broadcasted_iota(jnp.int32, (3 * PAD, LANES), 0)

    def fine_index(centre, outside, add):
        tap = inner - (centre + 1) % PAD
        return jnp.where((tap >= 0) & (tap < taps), tap, outside) + add

    index_y, index_x = fine_index(row, LANES - 1, 0), fine_index(col, LANES - 1, 0)
    tile_y, tile_x = tiles_of(row), tiles_of(col)
    row_four, col_four = spread(row, lane), spread(col, lane)
    cross_index_y, cross_index_x = fine_index(row_four, CROSS - 1, base), fine_index(col_four, CROSS - 1, base)
    cross_tile_y, cross_tile_x = tiles_of(row_four), tiles_of(col_four)
    first_tile = start_b // PAD

    def tile_in_strip(i, j, tile):
        return tile == (first_tile + (i - j)).astype(jnp.bfloat16)

    def one_band(b, carry):
        for k in range(comps):
            cut = pl.ds(k * LANES, LANES)
            placed = lookup(tmpl_y[k, pl.ds(b, 1), :], index_y)
            fine_y[b, :, cut] = placed.astype(jnp.bfloat16)
            fine_scaled[b, :, cut] = (placed * flux[k, pl.ds(b, 1), :]).astype(jnp.bfloat16)
            fine_x[:, cut] = lookup(tmpl_x[k, pl.ds(b, 1), :], index_x).astype(jnp.bfloat16)
        place(table_x.at[b], fine_x, 1, width // PAD, tile_x, 0, comps * LANES)
        for i in range(2):
            for k in range(comps):
                cut = pl.ds(k * LANES, LANES)
                value = jnp.zeros((PAD, LANES), jnp.bfloat16)
                for j in range(3):
                    value = jnp.where(tile_in_strip(i, j, tile_y), fine_scaled[b, pl.ds(PAD * j, PAD), cut], value)
                strip[pl.ds(PAD * i, PAD), cut] = value
        model = lax.dot_general(strip[...], table_x[b], NT, preferred_element_type=jnp.float32)
        send[pl.ds(b * 2 * PAD, 2 * PAD), :] = (-model).astype(jnp.bfloat16)
        shown = image[b].astype(jnp.float32)
        mine = jnp.where(top, model[PAD:], model[:PAD])
        row_at = pl.multiple_of(b * 2 * PAD + jnp.where(top, PAD, 0), PAD)
        send[pl.ds(row_at, PAD), :] = (shown - mine).astype(jnp.bfloat16)
        return carry

    copies[4].wait()
    lax.fori_loop(0, bands, one_band, 0)

    four_y = grouped(tmpl_y[...])
    four_x = grouped(tmpl_x[...])
    four_flux = grouped(jnp.where(lane < CROSS, flux[...], 0.0))
    for b in range(bands):
        for j in range(comps // 4):
            cut = pl.ds((b * (comps // 4) + j) * LANES, LANES)
            placed = lookup(four_y[j][b : b + 1], cross_index_y)
            cross_fine_y[:, cut] = placed.astype(jnp.bfloat16)
            cross_fine_scaled[:, cut] = (placed * four_flux[j][b : b + 1]).astype(jnp.bfloat16)
            cross_fine_x[:, cut] = lookup(four_x[j][b : b + 1], cross_index_x).astype(jnp.bfloat16)
            for side_at, tile in ((0, 0), (PAD, width // PAD + 1)):
                value = jnp.zeros((PAD, LANES), jnp.bfloat16)
                for p in range(3):
                    value = jnp.where(cross_tile_x == tile - p, cross_fine_x[pl.ds(PAD * p, PAD), cut], value)
                cross_x[pl.ds(b * CROSS + side_at, PAD), cut] = value
            for i in range(2):
                value = jnp.zeros((PAD, LANES), jnp.bfloat16)
                for p in range(3):
                    value = jnp.where(tile_in_strip(i, p, cross_tile_y), cross_fine_scaled[pl.ds(PAD * p, PAD), cut], value)
                cross_strip[pl.ds(PAD * i, PAD), cut] = value
    wide = -lax.dot_general(cross_strip[...], cross_x[...], NT, preferred_element_type=jnp.float32)
    send[pl.ds(bands * 2 * PAD, PAD), pl.ds(0, LANES)] = wide[:PAD].astype(jnp.bfloat16)
    send[pl.ds(bands * 2 * PAD, PAD), pl.ds(LANES, LANES)] = wide[PAD:].astype(jnp.bfloat16)


def render_kernel(
    scalars, pos, image, fine_y, fine_scaled, table_x, cross_fine_y, cross_fine_scaled, cross_x,
    field, side, send, table_y, cross_y, scaled, cross_scaled,
):
    bands, ext, width = field.shape
    height = ext - 2 * PAD
    lane = lax.broadcasted_iota(jnp.int32, (1, LANES), 1)
    row = pos[0:1, :]
    tile_y = tiles_of(row)
    cross_tile_y = tiles_of(spread(row, lane))

    def one_band(b, carry):
        place(scaled, fine_scaled.at[b], 0, ext // PAD, tile_y, 0, scaled.shape[1])
        model = lax.dot_general(scaled[...], table_x[b], NT, preferred_element_type=jnp.float32)
        field[b] = -model
        field[b, pl.ds(PAD, height), :] += image[b].astype(jnp.float32)
        place(table_y.at[b], fine_y.at[b], 0, ext // PAD, tile_y, 0, scaled.shape[1])
        return carry

    lax.fori_loop(0, bands, one_band, 0)
    place(cross_scaled, cross_fine_scaled, 0, ext // PAD, cross_tile_y, 0, cross_scaled.shape[1])
    place(cross_y, cross_fine_y, 0, ext // PAD, cross_tile_y, 0, cross_scaled.shape[1])
    side[...] = -lax.dot_general(cross_scaled[...], cross_x[...], NT, preferred_element_type=jnp.float32)
    start = starts(scalars, height)[0]
    for b in range(bands):
        send[pl.ds(b * 2 * PAD, 2 * PAD), :] = field[b, pl.ds(start, 2 * PAD), :].astype(jnp.bfloat16)
    wide = side[pl.ds(start, 2 * PAD), :].astype(jnp.bfloat16)
    send[pl.ds(bands * 2 * PAD, PAD), pl.ds(0, LANES)] = wide[:PAD]
    send[pl.ds(bands * 2 * PAD, PAD), pl.ds(LANES, LANES)] = wide[PAD:]


def add_rows(scalars, field, side, got_a, got_b):
    bands, ext = field.shape[0], field.shape[1]
    height = ext - 2 * PAD
    start_a, start_b = starts(scalars, height)
    for got, start in ((got_a, start_a), (got_b, start_b)):
        for b in range(bands):
            field[b, pl.ds(start, 2 * PAD), :] += got[pl.ds(b * 2 * PAD, 2 * PAD), :].astype(jnp.float32)
        side[pl.ds(start, PAD), :] += got[pl.ds(bands * 2 * PAD, PAD), pl.ds(0, LANES)].astype(jnp.float32)
        side[pl.ds(start + PAD, PAD), :] += got[pl.ds(bands * 2 * PAD, PAD), pl.ds(LANES, LANES)].astype(jnp.float32)


def column_kernel(scalars, field_in, side_in, got_a, got_b, field, side, send_a, send_b):
    bands, ext, width = field.shape
    field[...] = field_in[...]
    side[...] = side_in[...]
    add_rows(scalars, field, side, got_a, got_b)
    even = scalars[1] == 0
    lane = lax.broadcasted_iota(jnp.int32, (1, LANES), 1)
    to_left = side[...]
    to_right = side[...]
    for b in range(bands):
        low = pltpu.roll(field[b, :, pl.ds(0, LANES)], CROSS * b + PAD, axis=1)
        to_left = jnp.where((lane >= CROSS * b + PAD) & (lane < CROSS * (b + 1)), low, to_left)
        high = pltpu.roll(field[b, :, pl.ds(width - LANES, LANES)], CROSS * b + PAD, axis=1)
        to_right = jnp.where((lane >= CROSS * b) & (lane < CROSS * b + PAD), high, to_right)
    send_a[...] = jnp.where(even, to_right, to_left).astype(jnp.bfloat16)
    send_b[...] = jnp.where(even, to_left, to_right).astype(jnp.bfloat16)


def gradient_kernel(
    scalars, amp, field, side, got_a, got_b, table_y, table_x, cross_y, cross_x,
    updated, residual, total, gradient, sem,
):
    bands, ext, width = field.shape
    height = ext - 2 * PAD
    comps = amp.shape[0]
    even = scalars[1] == 0
    live = scalars[2]
    lane = lax.broadcasted_iota(jnp.int32, (1, LANES), 1)
    from_a, from_b = got_a[...].astype(jnp.float32), got_b[...].astype(jnp.float32)
    from_left = jnp.where(even, from_b, from_a)
    from_right = jnp.where(even, from_a, from_b)
    total[...] = field[...]
    for b in range(bands):
        low = pltpu.roll(from_left, LANES - CROSS * b - PAD, axis=1)
        total[b, :, pl.ds(0, LANES)] += jnp.where(lane < PAD, low, 0.0)
        high = pltpu.roll(from_right, LANES - CROSS * b - PAD, axis=1)
        total[b, :, pl.ds(width - LANES, LANES)] += jnp.where(lane >= LANES - PAD, high, 0.0)
    outer = side[...] + jnp.where(lane % CROSS < PAD, from_left, from_right)
    low_row, high_row, low_col, high_col = scalars[3], scalars[4], scalars[5], scalars[6]
    pixel_y = lax.broadcasted_iota(jnp.int32, (ext, LANES), 0)
    inside = (pixel_y >= low_row) & (pixel_y < high_row)
    inside = inside & (lane % CROSS >= low_col) & (lane % CROSS < high_col)
    outer = jnp.where(inside, outer, 0.0)

    @pl.when(low_row > 0)
    def _():
        total[:, pl.ds(0, PAD), :] = jnp.zeros((bands, PAD, width), jnp.float32)

    @pl.when(high_row < ext)
    def _():
        total[:, pl.ds(ext - PAD, PAD), :] = jnp.zeros((bands, PAD, width), jnp.float32)

    leaving = pltpu.make_async_copy(total.at[:, pl.ds(PAD, height), :], residual, sem)
    leaving.start()

    def one_band(b, carry):
        rounded = total[b].astype(jnp.bfloat16)
        for k in range(0, comps, 2):
            cut = pl.ds(k * LANES, 2 * LANES)
            inner = lax.dot_general(rounded, table_x[b, :, cut], NN, preferred_element_type=jnp.float32)
            summed = jnp.sum(inner * table_y[b, :, cut].astype(jnp.float32), axis=0, keepdims=True)
            gradient[k, pl.ds(b, 1), :] = summed[:, :LANES]
            gradient[k + 1, pl.ds(b, 1), :] = summed[:, LANES:]
        return carry

    lax.fori_loop(0, bands, one_band, 0)

    inner = lax.dot_general(outer.astype(jnp.bfloat16), cross_x[...], NN, preferred_element_type=jnp.float32)
    summed = jnp.sum(inner * cross_y[...].astype(jnp.float32), axis=0, keepdims=True)
    for b in range(bands):
        for j in range(comps // 4):
            start = (b * (comps // 4) + j) * LANES
            four = summed[:, start : start + LANES]
            for i in range(4):
                part = four if i == 0 else pltpu.roll(four, LANES - CROSS * i, axis=1)
                gradient[4 * j + i, b : b + 1, :] += jnp.where(lane < CROSS, part, 0.0)
    updated[...] = amp[...] + step_rate * jnp.where(lane < live, gradient[...], 0.0)
    leaving.wait()


SMEM = pl.BlockSpec(memory_space=pltpu.SMEM)
VMEM = pl.BlockSpec(memory_space=pltpu.VMEM)
HBM = pl.BlockSpec(memory_space=pltpu.HBM)
params = pltpu.CompilerParams(vmem_limit_bytes=16 << 20)


def swaps(axis, first):
    out = []
    for i in range(first, lax.axis_size(axis) - 1, 2):
        out += [(i, i + 1), (i + 1, i)]
    return out


def on_device(image, amplitude, positions, live, psf_rows, psf_cols):
    amp = jnp.swapaxes(amplitude[0, 0], 0, 1)
    psf_rows, psf_cols = jnp.swapaxes(psf_rows, 0, 1), jnp.swapaxes(psf_cols, 0, 1)
    bands, height, width = image.shape
    comps, slots = amp.shape[0], amp.shape[2]
    ext = height + 2 * PAD
    shape = jax.ShapeDtypeStruct
    f32, bf16 = jnp.float32, jnp.bfloat16
    region, tile = lax.axis_index("region"), lax.axis_index("tile")
    scalars = jnp.stack([
        region % 2,
        tile % 2,
        live[0, 0],
        jnp.where(region == 0, PAD, 0),
        jnp.where(region == lax.axis_size("region") - 1, ext - PAD, ext),
        jnp.where(tile == 0, PAD, 0),
        jnp.where(tile == lax.axis_size("tile") - 1, PAD, 2 * PAD),
    ]).astype(jnp.int32)
    rows_sent = bands * 2 * PAD + PAD
    table_width = comps * slots
    fine = shape((bands, 3 * PAD, table_width), bf16)
    cross_width = bands * comps * CROSS
    cross_fine = shape((3 * PAD, cross_width), bf16)
    centres = positions[:, 0, 0]
    send_b, fine_y, fine_scaled, table_x, cross_fine_y, cross_fine_scaled, cross_x = pl.pallas_call(
        strip_kernel,
        out_shape=[
            shape((rows_sent, width), bf16), fine, fine, shape((bands, width, table_width), bf16),
            cross_fine, cross_fine, shape((bands * CROSS, cross_width), bf16),
        ],
        in_specs=[SMEM] + [HBM] * 5,
        out_specs=[VMEM] * 7,
        scratch_shapes=[
            pltpu.VMEM(centres.shape, jnp.int32), pltpu.VMEM(amp.shape, f32),
            pltpu.VMEM(psf_rows.shape, bf16), pltpu.VMEM(psf_cols.shape, bf16),
            pltpu.VMEM((bands, PAD, width), bf16), pltpu.SemaphoreType.DMA((5,)),
            pltpu.VMEM((comps, bands, LANES), f32), pltpu.VMEM((comps, bands, LANES), f32),
            pltpu.VMEM((comps, bands, LANES), f32), pltpu.VMEM((3 * PAD, table_width), bf16),
            pltpu.VMEM((2 * PAD, table_width), bf16), pltpu.VMEM((2 * PAD, cross_width), bf16),
            pltpu.VMEM((3 * PAD, cross_width), bf16),
        ],
        compiler_params=params,
    )(scalars, *[pltpu.with_memory_space_constraint(x, pltpu.HBM) for x in (centres, amp, psf_rows, psf_cols, image)])
    got_b = lax.ppermute(send_b, "region", swaps("region", 1))
    field, side, send_a, table_y, cross_y = pl.pallas_call(
        render_kernel,
        out_shape=[
            shape((bands, ext, width), f32), shape((ext, LANES), f32), shape((rows_sent, width), bf16),
            shape((bands, ext, table_width), bf16), shape((ext, cross_width), bf16),
        ],
        in_specs=[SMEM] + [VMEM] * 8,
        out_specs=[VMEM] * 5,
        scratch_shapes=[pltpu.VMEM((ext, table_width), bf16), pltpu.VMEM((ext, cross_width), bf16)],
        compiler_params=params,
    )(scalars, centres, image, fine_y, fine_scaled, table_x, cross_fine_y, cross_fine_scaled, cross_x)
    got_a = lax.ppermute(send_a, "region", swaps("region", 0))
    field, side, send_a, send_b = pl.pallas_call(
        column_kernel,
        out_shape=[
            shape((bands, ext, width), f32), shape((ext, LANES), f32),
            shape((ext, LANES), bf16), shape((ext, LANES), bf16),
        ],
        in_specs=[SMEM] + [VMEM] * 4,
        out_specs=[VMEM] * 4,
        compiler_params=params,
    )(scalars, field, side, got_a, got_b)
    got_b = lax.ppermute(send_b, "tile", swaps("tile", 1))
    got_a = lax.ppermute(send_a, "tile", swaps("tile", 0))
    updated, residual = pl.pallas_call(
        gradient_kernel,
        out_shape=[shape(amp.shape, f32), shape(image.shape, f32)],
        in_specs=[SMEM] + [VMEM] * 9,
        out_specs=[VMEM, HBM],
        scratch_shapes=[
            pltpu.VMEM((bands, ext, width), f32), pltpu.VMEM((comps, bands, LANES), f32),
            pltpu.SemaphoreType.DMA,
        ],
        compiler_params=params,
    )(scalars, amp, field, side, got_a, got_b, table_y, table_x, cross_y, cross_x)
    return (jnp.swapaxes(updated, 0, 1)[None, None], residual)


def solution(mesh):
    in_specs = (
        P(None, "region", "tile"),
        P("region", "tile", None, None, None),
        P(None, "region", "tile", None),
        P("region", "tile"),
        P(),
        P(),
    )
    out_specs = (P("region", "tile", None, None, None), P(None, "region", "tile"))
    return jax.shard_map(
        on_device, mesh=mesh, in_specs=in_specs, out_specs=out_specs, check_vma=False
    )
```

```python
import jax
import jax.numpy as jnp
from jax import lax
from jax.experimental import pallas as pl
from jax.experimental.pallas import tpu as pltpu
from jax.sharding import PartitionSpec as P

step_rate = 0.05
PAD = 16
LANES = 128
CROSS = 32
NT = (((1,), (1,)), ((), ()))
NN = (((1,), (0,)), ((), ()))


def lookup(row, index):
    return jnp.take_along_axis(jnp.broadcast_to(row, index.shape), index, axis=1)


def grouped(value):
    out = []
    for j in range(value.shape[0] // 4):
        total = value[4 * j]
        for i in range(1, 4):
            total = total + pltpu.roll(value[4 * j + i], CROSS * i, axis=1)
        out.append(total)
    return out


def place(dst, src, first, count, tile_of, offset, lanes):
    for i in range(count):
        here = [tile_of == first + i - j for j in range(3)]
        for k in range(lanes // LANES):
            cut = pl.ds(k * LANES, LANES)
            value = jnp.zeros((PAD, LANES), jnp.bfloat16)
            for j in range(3):
                value = jnp.where(here[j], src[pl.ds(PAD * j, PAD), cut], value)
            dst[pl.ds(offset + PAD * i, PAD), cut] = value


def tiles_of(centre):
    return jnp.broadcast_to((centre + 1) // PAD, (PAD, LANES)).astype(jnp.bfloat16)


def spread(value, lane):
    first = jnp.where(lane < CROSS, value, 0)
    out = first
    for i in range(1, 4):
        out = out + pltpu.roll(first, CROSS * i, axis=1)
    return out


def starts(scalars, height):
    even = scalars[0] == 0
    start_a = pl.multiple_of(jnp.where(even, height, 0), 2 * PAD)
    start_b = pl.multiple_of(jnp.where(even, 0, height), 2 * PAD)
    return start_a, start_b


def sides(scalars, got_a, got_b):
    even = scalars[1] == 0
    from_a, from_b = got_a.astype(jnp.float32), got_b.astype(jnp.float32)
    return jnp.where(even, from_b, from_a), jnp.where(even, from_a, from_b)


def low_columns(from_left, b, lane):
    return jnp.where(lane < PAD, pltpu.roll(from_left, LANES - CROSS * b - PAD, axis=1), 0.0)


def high_columns(from_right, b, lane):
    return jnp.where(lane >= LANES - PAD, pltpu.roll(from_right, LANES - CROSS * b - PAD, axis=1), 0.0)


def render_kernel(
    scalars, pos_hbm, amp_hbm, psf_rows_hbm, psf_cols_hbm, image_hbm,
    send_a, send_b, field, side, fine_y, table_x, cross_fine_y, cross_x, tiles, amp,
    pos, psf_rows, psf_cols, image, sems, tmpl_y, tmpl_x, flux,
    fine_scaled, fine_x, scaled, cross_fine_scaled, cross_fine_x, cross_scaled,
):
    comps, bands, taps = psf_rows.shape
    ext, width = field.shape[1], field.shape[2]
    height = ext - 2 * PAD
    copies = [
        pltpu.make_async_copy(pos_hbm, pos, sems.at[0]),
        pltpu.make_async_copy(psf_cols_hbm, psf_cols, sems.at[1]),
        pltpu.make_async_copy(psf_rows_hbm, psf_rows, sems.at[2]),
        pltpu.make_async_copy(amp_hbm, amp, sems.at[3]),
        pltpu.make_async_copy(image_hbm, image, sems.at[4]),
    ]
    for copy in copies:
        copy.start()
    live = scalars[2]
    lane = lax.broadcasted_iota(jnp.int32, (1, LANES), 1)
    base = (lane // CROSS) * CROSS
    tmpl_y[...] = jnp.zeros_like(tmpl_y)
    tmpl_x[...] = jnp.zeros_like(tmpl_x)
    cross_x[...] = jnp.zeros_like(cross_x)
    for copy in copies[:4]:
        copy.wait()
    tmpl_y[:, :, :taps] = psf_rows[...].astype(jnp.float32)
    tmpl_x[:, :, :taps] = psf_cols[...].astype(jnp.float32)
    flux[...] = jnp.where(lane < live, amp[...], 0.0)
    row, col = pos[0:1, :], pos[1:2, :]
    inner = lax.broadcasted_iota(jnp.int32, (3 * PAD, LANES), 0)

    def fine_index(centre, outside, add):
        tap = inner - (centre + 1) % PAD
        return jnp.where((tap >= 0) & (tap < taps), tap, outside) + add

    index_y, index_x = fine_index(row, LANES - 1, 0), fine_index(col, LANES - 1, 0)
    tile_y, tile_x = tiles_of(row), tiles_of(col)
    row_four, col_four = spread(row, lane), spread(col, lane)
    cross_index_y, cross_index_x = fine_index(row_four, CROSS - 1, base), fine_index(col_four, CROSS - 1, base)
    cross_tile_y, cross_tile_x = tiles_of(row_four), tiles_of(col_four)
    tiles[0] = tile_y
    tiles[1] = cross_tile_y

    four_y = grouped(tmpl_y[...])
    four_x = grouped(tmpl_x[...])
    four_flux = grouped(jnp.where(lane < CROSS, flux[...], 0.0))
    for b in range(bands):
        for j in range(comps // 4):
            cut = pl.ds((b * (comps // 4) + j) * LANES, LANES)
            placed = lookup(four_y[j][b : b + 1], cross_index_y)
            cross_fine_y[:, cut] = placed.astype(jnp.bfloat16)
            cross_fine_scaled[:, cut] = (placed * four_flux[j][b : b + 1]).astype(jnp.bfloat16)
            cross_fine_x[:, cut] = lookup(four_x[j][b : b + 1], cross_index_x).astype(jnp.bfloat16)
            for side_at, tile in ((0, 0), (PAD, width // PAD + 1)):
                value = jnp.zeros((PAD, LANES), jnp.bfloat16)
                for p in range(3):
                    value = jnp.where(cross_tile_x == tile - p, cross_fine_x[pl.ds(PAD * p, PAD), cut], value)
                cross_x[pl.ds(b * CROSS + side_at, PAD), cut] = value
    place(cross_scaled, cross_fine_scaled, 0, ext // PAD, cross_tile_y, 0, cross_scaled.shape[1])
    side[...] = -lax.dot_general(cross_scaled[...], cross_x[...], NT, preferred_element_type=jnp.float32)

    def one_band(b, buffers):
        fine_scaled, fine_x, scaled = buffers
        for k in range(comps):
            cut = pl.ds(k * LANES, LANES)
            placed = lookup(tmpl_y[k, pl.ds(b, 1), :], index_y)
            fine_y[b, :, cut] = placed.astype(jnp.bfloat16)
            fine_scaled[:, cut] = (placed * flux[k, pl.ds(b, 1), :]).astype(jnp.bfloat16)
            fine_x[:, cut] = lookup(tmpl_x[k, pl.ds(b, 1), :], index_x).astype(jnp.bfloat16)
        place(table_x.at[b], fine_x, 1, width // PAD, tile_x, 0, comps * LANES)
        place(scaled, fine_scaled, 0, ext // PAD, tile_y, 0, comps * LANES)
        field[b] = -lax.dot_general(scaled[...], table_x[b], NT, preferred_element_type=jnp.float32)

    for b in range(bands):
        one_band(b, (fine_scaled.at[b], fine_x.at[b], scaled.at[b]))
    copies[4].wait()
    for b in range(bands):
        field[b, pl.ds(PAD, height), :] += image[b].astype(jnp.float32)
    to_left = side[...]
    to_right = side[...]
    for b in range(bands):
        low = pltpu.roll(field[b, :, pl.ds(0, LANES)], CROSS * b + PAD, axis=1)
        to_left = jnp.where((lane >= CROSS * b + PAD) & (lane < CROSS * (b + 1)), low, to_left)
        high = pltpu.roll(field[b, :, pl.ds(width - LANES, LANES)], CROSS * b + PAD, axis=1)
        to_right = jnp.where((lane >= CROSS * b) & (lane < CROSS * b + PAD), high, to_right)
    even = scalars[1] == 0
    send_a[...] = jnp.where(even, to_right, to_left).astype(jnp.bfloat16)
    send_b[...] = jnp.where(even, to_left, to_right).astype(jnp.bfloat16)


def place_kernel(tiles, fine_y, cross_fine_y, ready, table_y, cross_y, send):
    bands, ext, columns = table_y.shape
    tile_y, cross_tile_y = tiles[0], tiles[1]

    def one_band(b, carry):
        place(table_y.at[b], fine_y.at[b], 0, ext // PAD, tile_y, 0, columns)
        return carry

    send[...] = ready[...]
    lax.fori_loop(0, bands, one_band, 0)
    place(cross_y, cross_fine_y, 0, ext // PAD, cross_tile_y, 0, cross_y.shape[1])


def strip_kernel(scalars, field, side, got_a, got_b, send_a, send_b):
    bands, ext, width = field.shape
    lane = lax.broadcasted_iota(jnp.int32, (1, LANES), 1)
    for send, start in zip((send_a, send_b), starts(scalars, ext - 2 * PAD)):
        rows = pl.ds(start, 2 * PAD)
        from_left, from_right = sides(scalars, got_a[rows, :], got_b[rows, :])
        for b in range(bands):
            to = pl.ds(b * 2 * PAD, 2 * PAD)
            low = field[b, rows, pl.ds(0, LANES)] + low_columns(from_left, b, lane)
            high = field[b, rows, pl.ds(width - LANES, LANES)] + high_columns(from_right, b, lane)
            send[to, pl.ds(0, LANES)] = low.astype(jnp.bfloat16)
            send[to, pl.ds(width - LANES, LANES)] = high.astype(jnp.bfloat16)
        wide = side[rows, :] + jnp.where(lane % CROSS < PAD, from_left, from_right)
        wide = wide.astype(jnp.bfloat16)
        send[pl.ds(bands * 2 * PAD, PAD), pl.ds(0, LANES)] = wide[:PAD]
        send[pl.ds(bands * 2 * PAD, PAD), pl.ds(LANES, LANES)] = wide[PAD:]


def gradient_kernel(
    scalars, amp, field, side, cols_a, cols_b, rows_a, rows_b, table_y, table_x, cross_y, cross_x,
    updated, residual, total, outer, gradient, sem,
):
    bands, ext, width = field.shape
    height = ext - 2 * PAD
    comps = amp.shape[0]
    live = scalars[2]
    lane = lax.broadcasted_iota(jnp.int32, (1, LANES), 1)
    from_left, from_right = sides(scalars, cols_a[...], cols_b[...])
    for b in range(bands):
        total[b, :, pl.ds(0, LANES)] = field[b, :, pl.ds(0, LANES)] + low_columns(from_left, b, lane)
        total[b, :, pl.ds(LANES, LANES)] = field[b, :, pl.ds(LANES, LANES)] + high_columns(from_right, b, lane)
    outer[...] = side[...] + jnp.where(lane % CROSS < PAD, from_left, from_right)
    for got, start in zip((rows_a, rows_b), starts(scalars, height)):
        for b in range(bands):
            total[b, pl.ds(start, 2 * PAD), :] += got[pl.ds(b * 2 * PAD, 2 * PAD), :].astype(jnp.float32)
        extra = pl.ds(bands * 2 * PAD, PAD)
        outer[pl.ds(start, PAD), :] += got[extra, pl.ds(0, LANES)].astype(jnp.float32)
        outer[pl.ds(start + PAD, PAD), :] += got[extra, pl.ds(LANES, LANES)].astype(jnp.float32)
    leaving = pltpu.make_async_copy(total.at[:, pl.ds(PAD, height), :], residual, sem)
    leaving.start()

    low_row, high_row, low_col, high_col = scalars[3], scalars[4], scalars[5], scalars[6]
    pixel_y = lax.broadcasted_iota(jnp.int32, (ext, LANES), 0)
    inside = (pixel_y >= low_row) & (pixel_y < high_row)
    inside = inside & (lane % CROSS >= low_col) & (lane % CROSS < high_col)
    beyond = jnp.where(inside, outer[...], 0.0).astype(jnp.bfloat16)

    @pl.when(low_row > 0)
    def _():
        total[:, pl.ds(0, PAD), :] = jnp.zeros((bands, PAD, width), jnp.float32)

    @pl.when(high_row < ext)
    def _():
        total[:, pl.ds(ext - PAD, PAD), :] = jnp.zeros((bands, PAD, width), jnp.float32)

    def one_band(b, carry):
        rounded = total[b].astype(jnp.bfloat16)
        for k in range(0, comps, 2):
            cut = pl.ds(k * LANES, 2 * LANES)
            inner = lax.dot_general(rounded, table_x[b, :, cut], NN, preferred_element_type=jnp.float32)
            summed = jnp.sum(inner * table_y[b, :, cut].astype(jnp.float32), axis=0, keepdims=True)
            gradient[k, pl.ds(b, 1), :] = summed[:, :LANES]
            gradient[k + 1, pl.ds(b, 1), :] = summed[:, LANES:]
        return carry

    lax.fori_loop(0, bands, one_band, 0)

    inner = lax.dot_general(beyond, cross_x[...], NN, preferred_element_type=jnp.float32)
    summed = jnp.sum(inner * cross_y[...].astype(jnp.float32), axis=0, keepdims=True)
    for b in range(bands):
        for j in range(comps // 4):
            start = (b * (comps // 4) + j) * LANES
            four = summed[:, start : start + LANES]
            for i in range(4):
                part = four if i == 0 else pltpu.roll(four, LANES - CROSS * i, axis=1)
                gradient[4 * j + i, b : b + 1, :] += jnp.where(lane < CROSS, part, 0.0)
    updated[...] = amp[...] + step_rate * jnp.where(lane < live, gradient[...], 0.0)
    leaving.wait()


SMEM = pl.BlockSpec(memory_space=pltpu.SMEM)
VMEM = pl.BlockSpec(memory_space=pltpu.VMEM)
HBM = pl.BlockSpec(memory_space=pltpu.HBM)
params = pltpu.CompilerParams(vmem_limit_bytes=16 << 20)


def swaps(axis, first):
    out = []
    for i in range(first, lax.axis_size(axis) - 1, 2):
        out += [(i, i + 1), (i + 1, i)]
    return out


def on_device(image, amplitude, positions, live, psf_rows, psf_cols):
    amp = jnp.swapaxes(amplitude[0, 0], 0, 1)
    psf_rows, psf_cols = jnp.swapaxes(psf_rows, 0, 1), jnp.swapaxes(psf_cols, 0, 1)
    bands, height, width = image.shape
    comps, slots = amp.shape[0], amp.shape[2]
    ext = height + 2 * PAD
    shape = jax.ShapeDtypeStruct
    f32, bf16 = jnp.float32, jnp.bfloat16
    region, tile = lax.axis_index("region"), lax.axis_index("tile")
    scalars = jnp.stack([
        region % 2,
        tile % 2,
        live[0, 0],
        jnp.where(region == 0, PAD, 0),
        jnp.where(region == lax.axis_size("region") - 1, ext - PAD, ext),
        jnp.where(tile == 0, PAD, 0),
        jnp.where(tile == lax.axis_size("tile") - 1, PAD, 2 * PAD),
    ]).astype(jnp.int32)
    rows_sent = bands * 2 * PAD + PAD
    table_width = comps * slots
    cross_width = bands * comps * CROSS
    centres = positions[:, 0, 0]
    strip = shape((ext, LANES), bf16)
    (send_a, send_b, field, side, fine_y, table_x, cross_fine_y, cross_x, tiles, amp) = pl.pallas_call(
        render_kernel,
        out_shape=[
            strip, strip, shape((bands, ext, width), f32), shape((ext, LANES), f32),
            shape((bands, 3 * PAD, table_width), bf16), shape((bands, width, table_width), bf16),
            shape((3 * PAD, cross_width), bf16), shape((bands * CROSS, cross_width), bf16),
            shape((2, PAD, LANES), bf16), shape(amp.shape, f32),
        ],
        in_specs=[SMEM] + [HBM] * 5,
        out_specs=[VMEM] * 10,
        scratch_shapes=[
            pltpu.VMEM(centres.shape, jnp.int32),
            pltpu.VMEM(psf_rows.shape, bf16), pltpu.VMEM(psf_cols.shape, bf16),
            pltpu.VMEM(image.shape, bf16), pltpu.SemaphoreType.DMA((5,)),
            pltpu.VMEM((comps, bands, LANES), f32), pltpu.VMEM((comps, bands, LANES), f32),
            pltpu.VMEM((comps, bands, LANES), f32),
            pltpu.VMEM((4, 3 * PAD, table_width), bf16), pltpu.VMEM((4, 3 * PAD, table_width), bf16),
            pltpu.VMEM((4, ext, table_width), bf16),
            pltpu.VMEM((3 * PAD, cross_width), bf16), pltpu.VMEM((3 * PAD, cross_width), bf16),
            pltpu.VMEM((ext, cross_width), bf16),
        ],
        compiler_params=params,
    )(scalars, *[pltpu.with_memory_space_constraint(x, pltpu.HBM) for x in (centres, amp, psf_rows, psf_cols, image)])
    cols_b = lax.ppermute(send_b, "tile", swaps("tile", 1))
    table_y, cross_y, send_a = pl.pallas_call(
        place_kernel,
        out_shape=[shape((bands, ext, table_width), bf16), shape((ext, cross_width), bf16), strip],
        in_specs=[VMEM] * 4,
        out_specs=[VMEM] * 3,
        compiler_params=params,
    )(tiles, fine_y, cross_fine_y, send_a)
    cols_a = lax.ppermute(send_a, "tile", swaps("tile", 0))
    send_a, send_b = pl.pallas_call(
        strip_kernel,
        out_shape=[shape((rows_sent, width), bf16)] * 2,
        in_specs=[SMEM] + [VMEM] * 4,
        out_specs=[VMEM] * 2,
        compiler_params=params,
    )(scalars, field, side, cols_a, cols_b)
    rows_a = lax.ppermute(send_a, "region", swaps("region", 0))
    rows_b = lax.ppermute(send_b, "region", swaps("region", 1))
    updated, residual = pl.pallas_call(
        gradient_kernel,
        out_shape=[shape(amp.shape, f32), shape(image.shape, f32)],
        in_specs=[SMEM] + [VMEM] * 11,
        out_specs=[VMEM, HBM],
        scratch_shapes=[
            pltpu.VMEM((bands, ext, width), f32), pltpu.VMEM((ext, LANES), f32),
            pltpu.VMEM((comps, bands, LANES), f32), pltpu.SemaphoreType.DMA,
        ],
        compiler_params=params,
    )(scalars, amp, field, side, cols_a, cols_b, rows_a, rows_b, table_y, table_x, cross_y, cross_x)
    return (jnp.swapaxes(updated, 0, 1)[None, None], residual)


def solution(mesh):
    in_specs = (
        P(None, "region", "tile"),
        P("region", "tile", None, None, None),
        P(None, "region", "tile", None),
        P("region", "tile"),
        P(),
        P(),
    )
    out_specs = (P("region", "tile", None, None, None), P(None, "region", "tile"))
    return jax.shard_map(
        on_device, mesh=mesh, in_specs=in_specs, out_specs=out_specs, check_vma=False
    )
```

```python
import jax
import jax.numpy as jnp
from jax import lax
from jax.experimental import pallas as pl
from jax.experimental.pallas import tpu as pltpu
from jax.sharding import PartitionSpec as P

step_rate = 0.05
PAD = 16
LANES = 128
CROSS = 32
NT = (((1,), (1,)), ((), ()))
NN = (((1,), (0,)), ((), ()))


def lookup(row, index):
    return jnp.take_along_axis(jnp.broadcast_to(row, index.shape), index, axis=1)


def grouped(value):
    out = []
    for j in range(value.shape[0] // 4):
        total = value[4 * j]
        for i in range(1, 4):
            total = total + pltpu.roll(value[4 * j + i], CROSS * i, axis=1)
        out.append(total)
    return out


def place(dst, src, first, count, tile_of, offset, lanes):
    for i in range(count):
        here = [tile_of == first + i - j for j in range(3)]
        for k in range(lanes // LANES):
            cut = pl.ds(k * LANES, LANES)
            value = jnp.zeros((PAD, LANES), jnp.bfloat16)
            for j in range(3):
                value = jnp.where(here[j], src[pl.ds(PAD * j, PAD), cut], value)
            dst[pl.ds(offset + PAD * i, PAD), cut] = value


def tiles_of(centre):
    return jnp.broadcast_to((centre + 1) // PAD, (PAD, LANES)).astype(jnp.bfloat16)


def spread(value, lane):
    first = jnp.where(lane < CROSS, value, 0)
    out = first
    for i in range(1, 4):
        out = out + pltpu.roll(first, CROSS * i, axis=1)
    return out


def starts(scalars, height):
    even = scalars[0] == 0
    start_a = pl.multiple_of(jnp.where(even, height, 0), 2 * PAD)
    start_b = pl.multiple_of(jnp.where(even, 0, height), 2 * PAD)
    return start_a, start_b


def sides(scalars, got_a, got_b):
    even = scalars[1] == 0
    from_a, from_b = got_a.astype(jnp.float32), got_b.astype(jnp.float32)
    return jnp.where(even, from_b, from_a), jnp.where(even, from_a, from_b)


def low_columns(from_left, b, lane):
    return jnp.where(lane < PAD, pltpu.roll(from_left, LANES - CROSS * b - PAD, axis=1), 0.0)


def high_columns(from_right, b, lane):
    return jnp.where(lane >= LANES - PAD, pltpu.roll(from_right, LANES - CROSS * b - PAD, axis=1), 0.0)


def edge_kernel(
    scalars, pos_hbm, amp_hbm, psf_rows_hbm, psf_cols_hbm, image_hbm,
    send_a, send_b, fine_y, fine_scaled, table_x, cross_fine_y, cross_fine_scaled, cross_x, tiles, amp, image,
    pos, psf_rows, psf_cols, sems, tmpl_y, tmpl_x, flux, fine_x, strips, cross_fine_x, cross_strips,
):
    comps, bands, taps = psf_rows.shape
    height, width = image.shape[1], image.shape[2]
    even = scalars[0] == 0
    copies = [
        pltpu.make_async_copy(pos_hbm, pos, sems.at[0]),
        pltpu.make_async_copy(psf_cols_hbm, psf_cols, sems.at[1]),
        pltpu.make_async_copy(psf_rows_hbm, psf_rows, sems.at[2]),
        pltpu.make_async_copy(amp_hbm, amp, sems.at[3]),
        pltpu.make_async_copy(image_hbm, image, sems.at[4]),
    ]
    for copy in copies:
        copy.start()
    live = scalars[2]
    lane = lax.broadcasted_iota(jnp.int32, (1, LANES), 1)
    base = (lane // CROSS) * CROSS
    tmpl_y[...] = jnp.zeros_like(tmpl_y)
    tmpl_x[...] = jnp.zeros_like(tmpl_x)
    cross_x[...] = jnp.zeros_like(cross_x)
    for copy in copies[:4]:
        copy.wait()
    tmpl_y[:, :, :taps] = psf_rows[...].astype(jnp.float32)
    tmpl_x[:, :, :taps] = psf_cols[...].astype(jnp.float32)
    flux[...] = jnp.where(lane < live, amp[...], 0.0)
    row, col = pos[0:1, :], pos[1:2, :]
    inner = lax.broadcasted_iota(jnp.int32, (3 * PAD, LANES), 0)

    def fine_index(centre, outside, add):
        tap = inner - (centre + 1) % PAD
        return jnp.where((tap >= 0) & (tap < taps), tap, outside) + add

    index_y, index_x = fine_index(row, LANES - 1, 0), fine_index(col, LANES - 1, 0)
    tile_y, tile_x = tiles_of(row), tiles_of(col)
    row_four, col_four = spread(row, lane), spread(col, lane)
    cross_index_y, cross_index_x = fine_index(row_four, CROSS - 1, base), fine_index(col_four, CROSS - 1, base)
    cross_tile_y, cross_tile_x = tiles_of(row_four), tiles_of(col_four)
    tiles[0] = tile_y
    tiles[1] = cross_tile_y

    four_y = grouped(tmpl_y[...])
    four_x = grouped(tmpl_x[...])
    four_flux = grouped(jnp.where(lane < CROSS, flux[...], 0.0))
    for b in range(bands):
        for j in range(comps // 4):
            cut = pl.ds((b * (comps // 4) + j) * LANES, LANES)
            placed = lookup(four_y[j][b : b + 1], cross_index_y)
            cross_fine_y[:, cut] = placed.astype(jnp.bfloat16)
            cross_fine_scaled[:, cut] = (placed * four_flux[j][b : b + 1]).astype(jnp.bfloat16)
            cross_fine_x[:, cut] = lookup(four_x[j][b : b + 1], cross_index_x).astype(jnp.bfloat16)
            for side_at, tile in ((0, 0), (PAD, width // PAD + 1)):
                value = jnp.zeros((PAD, LANES), jnp.bfloat16)
                for p in range(3):
                    value = jnp.where(cross_tile_x == tile - p, cross_fine_x[pl.ds(PAD * p, PAD), cut], value)
                cross_x[pl.ds(b * CROSS + side_at, PAD), cut] = value

    def edges(dst, src, tile, columns):
        place(dst, src, 0, 2, tile, 0, columns)
        place(dst, src, height // PAD, 2, tile, 2 * PAD, columns)

    edges(cross_strips, cross_fine_scaled, cross_tile_y, cross_strips.shape[1])
    wide = -lax.dot_general(cross_strips[...], cross_x[...], NT, preferred_element_type=jnp.float32)

    def fill(to, top, bottom, part):
        send_a[to, part] = jnp.where(even, bottom, top).astype(jnp.bfloat16)
        send_b[to, part] = jnp.where(even, top, bottom).astype(jnp.bfloat16)

    extra = pl.ds(bands * 2 * PAD, PAD)
    fill(extra, wide[:PAD], wide[2 * PAD : 3 * PAD], pl.ds(0, LANES))
    fill(extra, wide[PAD : 2 * PAD], wide[3 * PAD :], pl.ds(LANES, LANES))
    copies[4].wait()
    for b in range(bands):
        for k in range(comps):
            cut = pl.ds(k * LANES, LANES)
            placed = lookup(tmpl_y[k, b : b + 1, :], index_y)
            fine_y[b, :, cut] = placed.astype(jnp.bfloat16)
            fine_scaled[b, :, cut] = (placed * flux[k, b : b + 1, :]).astype(jnp.bfloat16)
            fine_x[b, :, cut] = lookup(tmpl_x[k, b : b + 1, :], index_x).astype(jnp.bfloat16)
        place(table_x.at[b], fine_x.at[b], 1, width // PAD, tile_x, 0, comps * LANES)
        edges(strips.at[b], fine_scaled.at[b], tile_y, comps * LANES)
        model = -lax.dot_general(strips[b], table_x[b], NT, preferred_element_type=jnp.float32)
        top_in = image[b, pl.ds(0, PAD), :].astype(jnp.float32)
        bottom_in = image[b, pl.ds(height - PAD, PAD), :].astype(jnp.float32)
        every = pl.ds(0, width)
        fill(pl.ds(b * 2 * PAD, PAD), model[:PAD], model[2 * PAD : 3 * PAD] + bottom_in, every)
        fill(pl.ds(b * 2 * PAD + PAD, PAD), model[PAD : 2 * PAD] + top_in, model[3 * PAD :], every)


def pack(low, high, wide, lane):
    to_left = to_right = wide
    for b in range(len(low)):
        shift = CROSS * b + PAD
        to_left = jnp.where((lane >= shift) & (lane < shift + PAD), pltpu.roll(low[b], shift, axis=1), to_left)
        to_right = jnp.where((lane >= shift - PAD) & (lane < shift), pltpu.roll(high[b], shift, axis=1), to_right)
    return to_left, to_right


def render_kernel(
    image, tiles, fine_scaled, table_x, cross_fine_scaled, cross_x,
    field, side, to_left, to_right, scaled, cross_scaled,
):
    bands, ext, width = field.shape
    height = ext - 2 * PAD
    lane = lax.broadcasted_iota(jnp.int32, (1, LANES), 1)
    place(cross_scaled, cross_fine_scaled, 0, ext // PAD, tiles[1], 0, cross_scaled.shape[1])
    side[...] = -lax.dot_general(cross_scaled[...], cross_x[...], NT, preferred_element_type=jnp.float32)
    for b in range(bands):
        place(scaled.at[b], fine_scaled.at[b], 0, ext // PAD, tiles[0], 0, scaled.shape[2])
        model = lax.dot_general(scaled[b], table_x[b], NT, preferred_element_type=jnp.float32)
        field[b, pl.ds(0, PAD), :] = -model[:PAD]
        field[b, pl.ds(PAD, height), :] = image[b].astype(jnp.float32) - model[PAD : PAD + height]
        field[b, pl.ds(PAD + height, PAD), :] = -model[PAD + height :]
    low = [field[b, :, pl.ds(0, LANES)] for b in range(bands)]
    high = [field[b, :, pl.ds(width - LANES, LANES)] for b in range(bands)]
    to_left[...], to_right[...] = pack(low, high, side[...], lane)


def column_kernel(scalars, left_in, right_in, got_b, got_a, send_a, send_b, to_left, to_right):
    ext = left_in.shape[0]
    lane = lax.broadcasted_iota(jnp.int32, (1, LANES), 1)
    to_left[...] = left_in[...]
    to_right[...] = right_in[...]
    bands = (got_a.shape[0] - PAD) // (2 * PAD)
    width = got_a.shape[1]
    for got, start in zip((got_a, got_b), starts(scalars, ext - 2 * PAD)):
        value = got[...].astype(jnp.float32)
        low = [value[b * 2 * PAD : (b + 1) * 2 * PAD, :LANES] for b in range(bands)]
        high = [value[b * 2 * PAD : (b + 1) * 2 * PAD, width - LANES :] for b in range(bands)]
        extra = value[bands * 2 * PAD :]
        wide = jnp.concatenate([extra[:, :LANES], extra[:, LANES : 2 * LANES]], axis=0)
        left, right = pack(low, high, wide, lane)
        to_left[pl.ds(start, 2 * PAD), :] += left
        to_right[pl.ds(start, 2 * PAD), :] += right
    even = scalars[1] == 0
    send_a[...] = jnp.where(even, to_right[...], to_left[...]).astype(jnp.bfloat16)
    send_b[...] = jnp.where(even, to_left[...], to_right[...]).astype(jnp.bfloat16)


def place_kernel(tiles, fine_y, cross_fine_y, ready, table_y, cross_y, send):
    bands, ext, columns = table_y.shape
    tile_y, cross_tile_y = tiles[0], tiles[1]

    def one_band(b, carry):
        place(table_y.at[b], fine_y.at[b], 0, ext // PAD, tile_y, 0, columns)
        return carry

    send[...] = ready[...]
    lax.fori_loop(0, bands, one_band, 0)
    place(cross_y, cross_fine_y, 0, ext // PAD, cross_tile_y, 0, cross_y.shape[1])


def gradient_kernel(
    scalars, amp, field, side, cols_b, cols_a, rows_b, rows_a, table_y, table_x, cross_y, cross_x,
    updated, residual, total, outer, gradient, sem,
):
    bands, ext, width = field.shape
    height = ext - 2 * PAD
    comps = amp.shape[0]
    live = scalars[2]
    lane = lax.broadcasted_iota(jnp.int32, (1, LANES), 1)
    from_left, from_right = sides(scalars, cols_a[...], cols_b[...])
    for b in range(bands):
        total[b, :, pl.ds(0, LANES)] = field[b, :, pl.ds(0, LANES)] + low_columns(from_left, b, lane)
        total[b, :, pl.ds(LANES, LANES)] = field[b, :, pl.ds(LANES, LANES)] + high_columns(from_right, b, lane)
    outer[...] = side[...] + jnp.where(lane % CROSS < PAD, from_left, from_right)
    for got, start in zip((rows_a, rows_b), starts(scalars, height)):
        for b in range(bands):
            total[b, pl.ds(start, 2 * PAD), :] += got[pl.ds(b * 2 * PAD, 2 * PAD), :].astype(jnp.float32)
        extra = pl.ds(bands * 2 * PAD, PAD)
        outer[pl.ds(start, PAD), :] += got[extra, pl.ds(0, LANES)].astype(jnp.float32)
        outer[pl.ds(start + PAD, PAD), :] += got[extra, pl.ds(LANES, LANES)].astype(jnp.float32)
    leaving = pltpu.make_async_copy(total.at[:, pl.ds(PAD, height), :], residual, sem)
    leaving.start()

    low_row, high_row, low_col, high_col = scalars[3], scalars[4], scalars[5], scalars[6]
    pixel_y = lax.broadcasted_iota(jnp.int32, (ext, LANES), 0)
    inside = (pixel_y >= low_row) & (pixel_y < high_row)
    inside = inside & (lane % CROSS >= low_col) & (lane % CROSS < high_col)
    beyond = jnp.where(inside, outer[...], 0.0).astype(jnp.bfloat16)

    @pl.when(low_row > 0)
    def _():
        total[:, pl.ds(0, PAD), :] = jnp.zeros((bands, PAD, width), jnp.float32)

    @pl.when(high_row < ext)
    def _():
        total[:, pl.ds(ext - PAD, PAD), :] = jnp.zeros((bands, PAD, width), jnp.float32)

    def one_band(b, carry):
        rounded = total[b].astype(jnp.bfloat16)
        for k in range(0, comps, 2):
            cut = pl.ds(k * LANES, 2 * LANES)
            inner = lax.dot_general(rounded, table_x[b, :, cut], NN, preferred_element_type=jnp.float32)
            summed = jnp.sum(inner * table_y[b, :, cut].astype(jnp.float32), axis=0, keepdims=True)
            gradient[k, pl.ds(b, 1), :] = summed[:, :LANES]
            gradient[k + 1, pl.ds(b, 1), :] = summed[:, LANES:]
        return carry

    lax.fori_loop(0, bands, one_band, 0)

    inner = lax.dot_general(beyond, cross_x[...], NN, preferred_element_type=jnp.float32)
    summed = jnp.sum(inner * cross_y[...].astype(jnp.float32), axis=0, keepdims=True)
    for b in range(bands):
        for j in range(comps // 4):
            start = (b * (comps // 4) + j) * LANES
            four = summed[:, start : start + LANES]
            for i in range(4):
                part = four if i == 0 else pltpu.roll(four, LANES - CROSS * i, axis=1)
                gradient[4 * j + i, b : b + 1, :] += jnp.where(lane < CROSS, part, 0.0)
    updated[...] = amp[...] + step_rate * jnp.where(lane < live, gradient[...], 0.0)
    leaving.wait()


SMEM = pl.BlockSpec(memory_space=pltpu.SMEM)
VMEM = pl.BlockSpec(memory_space=pltpu.VMEM)
HBM = pl.BlockSpec(memory_space=pltpu.HBM)
params = pltpu.CompilerParams(vmem_limit_bytes=16 << 20)


def swaps(axis, first):
    out = []
    for i in range(first, lax.axis_size(axis) - 1, 2):
        out += [(i, i + 1), (i + 1, i)]
    return out


def on_device(image, amplitude, positions, live, psf_rows, psf_cols):
    amp = jnp.swapaxes(amplitude[0, 0], 0, 1)
    psf_rows, psf_cols = jnp.swapaxes(psf_rows, 0, 1), jnp.swapaxes(psf_cols, 0, 1)
    bands, height, width = image.shape
    comps, slots = amp.shape[0], amp.shape[2]
    ext = height + 2 * PAD
    shape = jax.ShapeDtypeStruct
    f32, bf16 = jnp.float32, jnp.bfloat16
    region, tile = lax.axis_index("region"), lax.axis_index("tile")
    scalars = jnp.stack([
        region % 2,
        tile % 2,
        live[0, 0],
        jnp.where(region == 0, PAD, 0),
        jnp.where(region == lax.axis_size("region") - 1, ext - PAD, ext),
        jnp.where(tile == 0, PAD, 0),
        jnp.where(tile == lax.axis_size("tile") - 1, PAD, 2 * PAD),
    ]).astype(jnp.int32)
    rows_sent = bands * 2 * PAD + PAD
    table_width = comps * slots
    cross_width = bands * comps * CROSS
    centres = positions[:, 0, 0]
    strip = shape((ext, LANES), bf16)
    fine = shape((bands, 3 * PAD, table_width), bf16)
    cross_fine = shape((3 * PAD, cross_width), bf16)
    (
        send_a, send_b, fine_y, fine_scaled, table_x, cross_fine_y, cross_fine_scaled, cross_x, tiles, amp, image,
    ) = pl.pallas_call(
        edge_kernel,
        out_shape=[
            shape((rows_sent, width), bf16), shape((rows_sent, width), bf16),
            fine, fine, shape((bands, width, table_width), bf16),
            cross_fine, cross_fine, shape((bands * CROSS, cross_width), bf16),
            shape((2, PAD, LANES), bf16), shape(amp.shape, f32), shape(image.shape, bf16),
        ],
        in_specs=[SMEM] + [HBM] * 5,
        out_specs=[VMEM] * 11,
        scratch_shapes=[
            pltpu.VMEM(centres.shape, jnp.int32),
            pltpu.VMEM(psf_rows.shape, bf16), pltpu.VMEM(psf_cols.shape, bf16), pltpu.SemaphoreType.DMA((5,)),
            pltpu.VMEM((comps, bands, LANES), f32), pltpu.VMEM((comps, bands, LANES), f32),
            pltpu.VMEM((comps, bands, LANES), f32), pltpu.VMEM((bands, 3 * PAD, table_width), bf16),
            pltpu.VMEM((bands, 4 * PAD, table_width), bf16), pltpu.VMEM((3 * PAD, cross_width), bf16),
            pltpu.VMEM((4 * PAD, cross_width), bf16),
        ],
        compiler_params=params,
    )(scalars, *[pltpu.with_memory_space_constraint(x, pltpu.HBM) for x in (centres, amp, psf_rows, psf_cols, image)])
    rows_b = lax.ppermute(send_b, "region", swaps("region", 1))
    rows_a = lax.ppermute(send_a, "region", swaps("region", 0))
    field, side, to_left, to_right = pl.pallas_call(
        render_kernel,
        out_shape=[
            shape((bands, ext, width), f32), shape((ext, LANES), f32),
            shape((ext, LANES), f32), shape((ext, LANES), f32),
        ],
        in_specs=[VMEM] * 6,
        out_specs=[VMEM] * 4,
        scratch_shapes=[pltpu.VMEM((bands, ext, table_width), bf16), pltpu.VMEM((ext, cross_width), bf16)],
        compiler_params=params,
    )(image, tiles, fine_scaled, table_x, cross_fine_scaled, cross_x)
    send_a, send_b = pl.pallas_call(
        column_kernel,
        out_shape=[strip, strip],
        in_specs=[SMEM] + [VMEM] * 4,
        out_specs=[VMEM] * 2,
        scratch_shapes=[pltpu.VMEM((ext, LANES), f32), pltpu.VMEM((ext, LANES), f32)],
        compiler_params=params,
    )(scalars, to_left, to_right, rows_b, rows_a)
    cols_b = lax.ppermute(send_b, "tile", swaps("tile", 1))
    table_y, cross_y, send_a = pl.pallas_call(
        place_kernel,
        out_shape=[shape((bands, ext, table_width), bf16), shape((ext, cross_width), bf16), strip],
        in_specs=[VMEM] * 4,
        out_specs=[VMEM] * 3,
        compiler_params=params,
    )(tiles, fine_y, cross_fine_y, send_a)
    cols_a = lax.ppermute(send_a, "tile", swaps("tile", 0))
    updated, residual = pl.pallas_call(
        gradient_kernel,
        out_shape=[shape(amp.shape, f32), shape(image.shape, f32)],
        in_specs=[SMEM] + [VMEM] * 11,
        out_specs=[VMEM, HBM],
        scratch_shapes=[
            pltpu.VMEM((bands, ext, width), f32), pltpu.VMEM((ext, LANES), f32),
            pltpu.VMEM((comps, bands, LANES), f32), pltpu.SemaphoreType.DMA,
        ],
        compiler_params=params,
    )(scalars, amp, field, side, cols_b, cols_a, rows_b, rows_a, table_y, table_x, cross_y, cross_x)
    return (jnp.swapaxes(updated, 0, 1)[None, None], residual)


def solution(mesh):
    in_specs = (
        P(None, "region", "tile"),
        P("region", "tile", None, None, None),
        P(None, "region", "tile", None),
        P("region", "tile"),
        P(),
        P(),
    )
    out_specs = (P("region", "tile", None, None, None), P(None, "region", "tile"))
    return jax.shard_map(
        on_device, mesh=mesh, in_specs=in_specs, out_specs=out_specs, check_vma=False
    )
```

```python
import jax
import jax.numpy as jnp
from jax import lax
from jax.experimental import pallas as pl
from jax.experimental.pallas import tpu as pltpu
from jax.sharding import PartitionSpec as P

step_rate = 0.05
PAD = 16
LANES = 128
CROSS = 32
NT = (((1,), (1,)), ((), ()))
NN = (((1,), (0,)), ((), ()))


def lookup(row, index):
    return jnp.take_along_axis(jnp.broadcast_to(row, index.shape), index, axis=1)


def grouped(value):
    out = []
    for j in range(value.shape[0] // 4):
        total = value[4 * j]
        for i in range(1, 4):
            total = total + pltpu.roll(value[4 * j + i], CROSS * i, axis=1)
        out.append(total)
    return out


def place(dst, src, first, count, tile_of, offset, lanes):
    for i in range(count):
        here = [tile_of == first + i - j for j in range(3)]
        for k in range(lanes // LANES):
            cut = pl.ds(k * LANES, LANES)
            value = jnp.zeros((PAD, LANES), jnp.bfloat16)
            for j in range(3):
                value = jnp.where(here[j], src[pl.ds(PAD * j, PAD), cut], value)
            dst[pl.ds(offset + PAD * i, PAD), cut] = value


def tiles_of(centre):
    return jnp.broadcast_to((centre + 1) // PAD, (PAD, LANES)).astype(jnp.bfloat16)


def spread(value, lane):
    first = jnp.where(lane < CROSS, value, 0)
    out = first
    for i in range(1, 4):
        out = out + pltpu.roll(first, CROSS * i, axis=1)
    return out


def starts(scalars, height):
    even = scalars[0] == 0
    start_a = pl.multiple_of(jnp.where(even, height, 0), 2 * PAD)
    start_b = pl.multiple_of(jnp.where(even, 0, height), 2 * PAD)
    return start_a, start_b


def sides(scalars, got_a, got_b):
    even = scalars[1] == 0
    from_a, from_b = got_a.astype(jnp.float32), got_b.astype(jnp.float32)
    return jnp.where(even, from_b, from_a), jnp.where(even, from_a, from_b)


def low_columns(from_left, b, lane):
    return jnp.where(lane < PAD, pltpu.roll(from_left, LANES - CROSS * b - PAD, axis=1), 0.0)


def high_columns(from_right, b, lane):
    return jnp.where(lane >= LANES - PAD, pltpu.roll(from_right, LANES - CROSS * b - PAD, axis=1), 0.0)


def edge_kernel(
    scalars, pos_hbm, amp_hbm, psf_rows_hbm, psf_cols_hbm, image_hbm,
    send_a, send_b, fine_y, fine_scaled, table_x, cross_fine_y, cross_fine_scaled, cross_x, tiles, amp, image,
    pos, psf_rows, psf_cols, sems, tmpl_y, tmpl_x, flux, fine_x, strips, cross_fine_x, cross_strips,
):
    comps, bands, taps = psf_rows.shape
    height, width = image.shape[1], image.shape[2]
    even = scalars[0] == 0
    copies = [
        pltpu.make_async_copy(pos_hbm, pos, sems.at[0]),
        pltpu.make_async_copy(psf_cols_hbm, psf_cols, sems.at[1]),
        pltpu.make_async_copy(psf_rows_hbm, psf_rows, sems.at[2]),
        pltpu.make_async_copy(amp_hbm, amp, sems.at[3]),
        pltpu.make_async_copy(image_hbm, image, sems.at[4]),
    ]
    for copy in copies:
        copy.start()
    live = scalars[2]
    lane = lax.broadcasted_iota(jnp.int32, (1, LANES), 1)
    base = (lane // CROSS) * CROSS
    tmpl_y[...] = jnp.zeros_like(tmpl_y)
    tmpl_x[...] = jnp.zeros_like(tmpl_x)
    cross_x[...] = jnp.zeros_like(cross_x)
    for copy in copies[:4]:
        copy.wait()
    tmpl_y[:, :, :taps] = psf_rows[...].astype(jnp.float32)
    tmpl_x[:, :, :taps] = psf_cols[...].astype(jnp.float32)
    flux[...] = jnp.where(lane < live, amp[...], 0.0)
    row, col = pos[0:1, :], pos[1:2, :]
    inner = lax.broadcasted_iota(jnp.int32, (3 * PAD, LANES), 0)

    def fine_index(centre, outside, add):
        tap = inner - (centre + 1) % PAD
        return jnp.where((tap >= 0) & (tap < taps), tap, outside) + add

    index_y, index_x = fine_index(row, LANES - 1, 0), fine_index(col, LANES - 1, 0)
    tile_y, tile_x = tiles_of(row), tiles_of(col)
    row_four, col_four = spread(row, lane), spread(col, lane)
    cross_index_y, cross_index_x = fine_index(row_four, CROSS - 1, base), fine_index(col_four, CROSS - 1, base)
    cross_tile_y, cross_tile_x = tiles_of(row_four), tiles_of(col_four)
    tiles[0] = tile_y
    tiles[1] = cross_tile_y

    four_y = grouped(tmpl_y[...])
    four_x = grouped(tmpl_x[...])
    four_flux = grouped(jnp.where(lane < CROSS, flux[...], 0.0))
    for b in range(bands):
        for j in range(comps // 4):
            cut = pl.ds((b * (comps // 4) + j) * LANES, LANES)
            placed = lookup(four_y[j][b : b + 1], cross_index_y)
            cross_fine_y[:, cut] = placed.astype(jnp.bfloat16)
            cross_fine_scaled[:, cut] = (placed * four_flux[j][b : b + 1]).astype(jnp.bfloat16)
            cross_fine_x[:, cut] = lookup(four_x[j][b : b + 1], cross_index_x).astype(jnp.bfloat16)
            for side_at, tile in ((0, 0), (PAD, width // PAD + 1)):
                value = jnp.zeros((PAD, LANES), jnp.bfloat16)
                for p in range(3):
                    value = jnp.where(cross_tile_x == tile - p, cross_fine_x[pl.ds(PAD * p, PAD), cut], value)
                cross_x[pl.ds(b * CROSS + side_at, PAD), cut] = value

    def edges(dst, src, tile, columns):
        place(dst, src, 0, 2, tile, 0, columns)
        place(dst, src, height // PAD, 2, tile, 2 * PAD, columns)

    edges(cross_strips, cross_fine_scaled, cross_tile_y, cross_strips.shape[1])
    wide = -lax.dot_general(cross_strips[...], cross_x[...], NT, preferred_element_type=jnp.float32)

    def fill(to, top, bottom, part):
        send_a[to, part] = jnp.where(even, bottom, top).astype(jnp.bfloat16)
        send_b[to, part] = jnp.where(even, top, bottom).astype(jnp.bfloat16)

    extra = pl.ds(bands * 2 * PAD, PAD)
    fill(extra, wide[:PAD], wide[2 * PAD : 3 * PAD], pl.ds(0, LANES))
    fill(extra, wide[PAD : 2 * PAD], wide[3 * PAD :], pl.ds(LANES, LANES))
    copies[4].wait()
    for b in range(bands):
        for k in range(comps):
            cut = pl.ds(k * LANES, LANES)
            placed = lookup(tmpl_y[k, b : b + 1, :], index_y)
            fine_y[b, :, cut] = placed.astype(jnp.bfloat16)
            fine_scaled[b, :, cut] = (placed * flux[k, b : b + 1, :]).astype(jnp.bfloat16)
            fine_x[b, :, cut] = lookup(tmpl_x[k, b : b + 1, :], index_x).astype(jnp.bfloat16)
        place(table_x.at[b], fine_x.at[b], 1, width // PAD, tile_x, 0, comps * LANES)
        edges(strips.at[b], fine_scaled.at[b], tile_y, comps * LANES)
        model = -lax.dot_general(strips[b], table_x[b], NT, preferred_element_type=jnp.float32)
        top_in = image[b, pl.ds(0, PAD), :].astype(jnp.float32)
        bottom_in = image[b, pl.ds(height - PAD, PAD), :].astype(jnp.float32)
        every = pl.ds(0, width)
        fill(pl.ds(b * 2 * PAD, PAD), model[:PAD], model[2 * PAD : 3 * PAD] + bottom_in, every)
        fill(pl.ds(b * 2 * PAD + PAD, PAD), model[PAD : 2 * PAD] + top_in, model[3 * PAD :], every)


def pack(low, high, wide, lane):
    to_left = to_right = wide
    for b in range(len(low)):
        shift = CROSS * b + PAD
        to_left = jnp.where((lane >= shift) & (lane < shift + PAD), pltpu.roll(low[b], shift, axis=1), to_left)
        to_right = jnp.where((lane >= shift - PAD) & (lane < shift), pltpu.roll(high[b], shift, axis=1), to_right)
    return to_left, to_right


def render_kernel(
    image, tiles, fine_scaled, table_x, cross_fine_scaled, cross_x,
    field, side, to_left, to_right, scaled, cross_scaled,
):
    bands, ext, width = field.shape
    height = ext - 2 * PAD
    lane = lax.broadcasted_iota(jnp.int32, (1, LANES), 1)
    place(cross_scaled, cross_fine_scaled, 0, ext // PAD, tiles[1], 0, cross_scaled.shape[1])
    side[...] = -lax.dot_general(cross_scaled[...], cross_x[...], NT, preferred_element_type=jnp.float32)
    for b in range(bands):
        place(scaled.at[b], fine_scaled.at[b], 0, ext // PAD, tiles[0], 0, scaled.shape[2])
        model = lax.dot_general(scaled[b], table_x[b], NT, preferred_element_type=jnp.float32)
        field[b, pl.ds(0, PAD), :] = -model[:PAD]
        field[b, pl.ds(PAD, height), :] = image[b].astype(jnp.float32) - model[PAD : PAD + height]
        field[b, pl.ds(PAD + height, PAD), :] = -model[PAD + height :]
    low = [field[b, :, pl.ds(0, LANES)] for b in range(bands)]
    high = [field[b, :, pl.ds(width - LANES, LANES)] for b in range(bands)]
    to_left[...], to_right[...] = pack(low, high, side[...], lane)


def column_kernel(scalars, left_in, right_in, got_b, got_a, send_a, send_b, to_left, to_right):
    ext = left_in.shape[0]
    lane = lax.broadcasted_iota(jnp.int32, (1, LANES), 1)
    to_left[...] = left_in[...]
    to_right[...] = right_in[...]
    bands = (got_a.shape[0] - PAD) // (2 * PAD)
    width = got_a.shape[1]
    for got, start in zip((got_a, got_b), starts(scalars, ext - 2 * PAD)):
        value = got[...].astype(jnp.float32)
        low = [value[b * 2 * PAD : (b + 1) * 2 * PAD, :LANES] for b in range(bands)]
        high = [value[b * 2 * PAD : (b + 1) * 2 * PAD, width - LANES :] for b in range(bands)]
        extra = value[bands * 2 * PAD :]
        wide = jnp.concatenate([extra[:, :LANES], extra[:, LANES : 2 * LANES]], axis=0)
        left, right = pack(low, high, wide, lane)
        to_left[pl.ds(start, 2 * PAD), :] += left
        to_right[pl.ds(start, 2 * PAD), :] += right
    even = scalars[1] == 0
    send_a[...] = jnp.where(even, to_right[...], to_left[...]).astype(jnp.bfloat16)
    send_b[...] = jnp.where(even, to_left[...], to_right[...]).astype(jnp.bfloat16)


def place_kernel(tiles, fine_y, cross_fine_y, ready, table_y, cross_y):
    bands, ext, columns = table_y.shape
    tile_y, cross_tile_y = tiles[0], tiles[1]

    def one_band(b, carry):
        place(table_y.at[b], fine_y.at[b], 0, ext // PAD, tile_y, 0, columns)
        return carry

    lax.fori_loop(0, bands, one_band, 0)
    place(cross_y, cross_fine_y, 0, ext // PAD, cross_tile_y, 0, cross_y.shape[1])


def gradient_kernel(
    scalars, amp, field, side, cols_b, cols_a, rows_b, rows_a, table_y, table_x, cross_y, cross_x,
    updated, residual, total, outer, gradient, sem,
):
    bands, ext, width = field.shape
    height = ext - 2 * PAD
    comps = amp.shape[0]
    live = scalars[2]
    lane = lax.broadcasted_iota(jnp.int32, (1, LANES), 1)
    from_left, from_right = sides(scalars, cols_a[...], cols_b[...])
    for b in range(bands):
        total[b, :, pl.ds(0, LANES)] = field[b, :, pl.ds(0, LANES)] + low_columns(from_left, b, lane)
        total[b, :, pl.ds(LANES, LANES)] = field[b, :, pl.ds(LANES, LANES)] + high_columns(from_right, b, lane)
    outer[...] = side[...] + jnp.where(lane % CROSS < PAD, from_left, from_right)
    for got, start in zip((rows_a, rows_b), starts(scalars, height)):
        for b in range(bands):
            total[b, pl.ds(start, 2 * PAD), :] += got[pl.ds(b * 2 * PAD, 2 * PAD), :].astype(jnp.float32)
        extra = pl.ds(bands * 2 * PAD, PAD)
        outer[pl.ds(start, PAD), :] += got[extra, pl.ds(0, LANES)].astype(jnp.float32)
        outer[pl.ds(start + PAD, PAD), :] += got[extra, pl.ds(LANES, LANES)].astype(jnp.float32)
    leaving = pltpu.make_async_copy(total.at[:, pl.ds(PAD, height), :], residual, sem)
    leaving.start()

    low_row, high_row, low_col, high_col = scalars[3], scalars[4], scalars[5], scalars[6]
    pixel_y = lax.broadcasted_iota(jnp.int32, (ext, LANES), 0)
    inside = (pixel_y >= low_row) & (pixel_y < high_row)
    inside = inside & (lane % CROSS >= low_col) & (lane % CROSS < high_col)
    beyond = jnp.where(inside, outer[...], 0.0).astype(jnp.bfloat16)

    total[:, pl.ds(0, PAD), :] = jnp.where(low_row > 0, 0.0, total[:, pl.ds(0, PAD), :])
    total[:, pl.ds(ext - PAD, PAD), :] = jnp.where(high_row < ext, 0.0, total[:, pl.ds(ext - PAD, PAD), :])
    for b in range(bands):
        rounded = total[b].astype(jnp.bfloat16)
        for k in range(0, comps, 2):
            cut = pl.ds(k * LANES, 2 * LANES)
            inner = lax.dot_general(rounded, table_x[b, :, cut], NN, preferred_element_type=jnp.float32)
            summed = jnp.sum(inner * table_y[b, :, cut].astype(jnp.float32), axis=0, keepdims=True)
            gradient[k, b : b + 1, :] = summed[:, :LANES]
            gradient[k + 1, b : b + 1, :] = summed[:, LANES:]

    inner = lax.dot_general(beyond, cross_x[...], NN, preferred_element_type=jnp.float32)
    summed = jnp.sum(inner * cross_y[...].astype(jnp.float32), axis=0, keepdims=True)
    for b in range(bands):
        for j in range(comps // 4):
            start = (b * (comps // 4) + j) * LANES
            four = summed[:, start : start + LANES]
            for i in range(4):
                part = four if i == 0 else pltpu.roll(four, LANES - CROSS * i, axis=1)
                gradient[4 * j + i, b : b + 1, :] += jnp.where(lane < CROSS, part, 0.0)
    updated[...] = amp[...] + step_rate * jnp.where(lane < live, gradient[...], 0.0)
    leaving.wait()


SMEM = pl.BlockSpec(memory_space=pltpu.SMEM)
VMEM = pl.BlockSpec(memory_space=pltpu.VMEM)
HBM = pl.BlockSpec(memory_space=pltpu.HBM)
params = pltpu.CompilerParams(vmem_limit_bytes=16 << 20)


def swaps(axis, first):
    out = []
    for i in range(first, lax.axis_size(axis) - 1, 2):
        out += [(i, i + 1), (i + 1, i)]
    return out


def on_device(image, amplitude, positions, live, psf_rows, psf_cols):
    amp = jnp.swapaxes(amplitude[0, 0], 0, 1)
    psf_rows, psf_cols = jnp.swapaxes(psf_rows, 0, 1), jnp.swapaxes(psf_cols, 0, 1)
    bands, height, width = image.shape
    comps, slots = amp.shape[0], amp.shape[2]
    ext = height + 2 * PAD
    shape = jax.ShapeDtypeStruct
    f32, bf16 = jnp.float32, jnp.bfloat16
    region, tile = lax.axis_index("region"), lax.axis_index("tile")
    scalars = jnp.stack([
        region % 2,
        tile % 2,
        live[0, 0],
        jnp.where(region == 0, PAD, 0),
        jnp.where(region == lax.axis_size("region") - 1, ext - PAD, ext),
        jnp.where(tile == 0, PAD, 0),
        jnp.where(tile == lax.axis_size("tile") - 1, PAD, 2 * PAD),
    ]).astype(jnp.int32)
    rows_sent = bands * 2 * PAD + PAD
    table_width = comps * slots
    cross_width = bands * comps * CROSS
    centres = positions[:, 0, 0]
    strip = shape((ext, LANES), bf16)
    fine = shape((bands, 3 * PAD, table_width), bf16)
    cross_fine = shape((3 * PAD, cross_width), bf16)
    (
        send_a, send_b, fine_y, fine_scaled, table_x, cross_fine_y, cross_fine_scaled, cross_x, tiles, amp, image,
    ) = pl.pallas_call(
        edge_kernel,
        out_shape=[
            shape((rows_sent, width), bf16), shape((rows_sent, width), bf16),
            fine, fine, shape((bands, width, table_width), bf16),
            cross_fine, cross_fine, shape((bands * CROSS, cross_width), bf16),
            shape((2, PAD, LANES), bf16), shape(amp.shape, f32), shape(image.shape, bf16),
        ],
        in_specs=[SMEM] + [HBM] * 5,
        out_specs=[VMEM] * 11,
        scratch_shapes=[
            pltpu.VMEM(centres.shape, jnp.int32),
            pltpu.VMEM(psf_rows.shape, bf16), pltpu.VMEM(psf_cols.shape, bf16), pltpu.SemaphoreType.DMA((5,)),
            pltpu.VMEM((comps, bands, LANES), f32), pltpu.VMEM((comps, bands, LANES), f32),
            pltpu.VMEM((comps, bands, LANES), f32), pltpu.VMEM((bands, 3 * PAD, table_width), bf16),
            pltpu.VMEM((bands, 4 * PAD, table_width), bf16), pltpu.VMEM((3 * PAD, cross_width), bf16),
            pltpu.VMEM((4 * PAD, cross_width), bf16),
        ],
        compiler_params=params,
    )(scalars, *[pltpu.with_memory_space_constraint(x, pltpu.HBM) for x in (centres, amp, psf_rows, psf_cols, image)])
    rows_b = lax.ppermute(send_b, "region", swaps("region", 1))
    rows_a = lax.ppermute(send_a, "region", swaps("region", 0))
    field, side, to_left, to_right = pl.pallas_call(
        render_kernel,
        out_shape=[
            shape((bands, ext, width), f32), shape((ext, LANES), f32),
            shape((ext, LANES), f32), shape((ext, LANES), f32),
        ],
        in_specs=[VMEM] * 6,
        out_specs=[VMEM] * 4,
        scratch_shapes=[pltpu.VMEM((bands, ext, table_width), bf16), pltpu.VMEM((ext, cross_width), bf16)],
        compiler_params=params,
    )(image, tiles, fine_scaled, table_x, cross_fine_scaled, cross_x)
    send_a, send_b = pl.pallas_call(
        column_kernel,
        out_shape=[strip, strip],
        in_specs=[SMEM] + [VMEM] * 4,
        out_specs=[VMEM] * 2,
        scratch_shapes=[pltpu.VMEM((ext, LANES), f32), pltpu.VMEM((ext, LANES), f32)],
        compiler_params=params,
    )(scalars, to_left, to_right, rows_b, rows_a)
    cols_b = lax.ppermute(send_b, "tile", swaps("tile", 1))
    cols_a = lax.ppermute(send_a, "tile", swaps("tile", 0))
    table_y, cross_y = pl.pallas_call(
        place_kernel,
        out_shape=[shape((bands, ext, table_width), bf16), shape((ext, cross_width), bf16)],
        in_specs=[VMEM] * 4,
        out_specs=[VMEM] * 2,
        compiler_params=params,
    )(tiles, fine_y, cross_fine_y, send_a)
    updated, residual = pl.pallas_call(
        gradient_kernel,
        out_shape=[shape(amp.shape, f32), shape(image.shape, f32)],
        in_specs=[SMEM] + [VMEM] * 11,
        out_specs=[VMEM, HBM],
        scratch_shapes=[
            pltpu.VMEM((bands, ext, width), f32), pltpu.VMEM((ext, LANES), f32),
            pltpu.VMEM((comps, bands, LANES), f32), pltpu.SemaphoreType.DMA,
        ],
        compiler_params=params,
    )(scalars, amp, field, side, cols_b, cols_a, rows_b, rows_a, table_y, table_x, cross_y, cross_x)
    return (jnp.swapaxes(updated, 0, 1)[None, None], residual)


def solution(mesh):
    in_specs = (
        P(None, "region", "tile"),
        P("region", "tile", None, None, None),
        P(None, "region", "tile", None),
        P("region", "tile"),
        P(),
        P(),
    )
    out_specs = (P("region", "tile", None, None, None), P(None, "region", "tile"))
    return jax.shard_map(
        on_device, mesh=mesh, in_specs=in_specs, out_specs=out_specs, check_vma=False
    )
```

```python
import jax
import jax.numpy as jnp
from jax import lax
from jax.experimental import pallas as pl
from jax.experimental.pallas import tpu as pltpu
from jax.sharding import PartitionSpec as P

step_rate = 0.05
PAD = 16
LANES = 128
CROSS = 32
NT = (((1,), (1,)), ((), ()))
NN = (((1,), (0,)), ((), ()))


def lookup(row, index):
    return jnp.take_along_axis(jnp.broadcast_to(row, index.shape), index, axis=1)


def grouped(value):
    out = []
    for j in range(value.shape[0] // 4):
        total = value[4 * j]
        for i in range(1, 4):
            total = total + pltpu.roll(value[4 * j + i], CROSS * i, axis=1)
        out.append(total)
    return out


def place(dst, src, first, count, tile_of, offset, lanes):
    for i in range(count):
        here = [tile_of == first + i - j for j in range(3)]
        for k in range(lanes // LANES):
            cut = pl.ds(k * LANES, LANES)
            value = jnp.zeros((PAD, LANES), jnp.bfloat16)
            for j in range(3):
                value = jnp.where(here[j], src[pl.ds(PAD * j, PAD), cut], value)
            dst[pl.ds(offset + PAD * i, PAD), cut] = value


def tiles_of(centre):
    return jnp.broadcast_to((centre + 1) // PAD, (PAD, LANES)).astype(jnp.bfloat16)


def spread(value, lane):
    first = jnp.where(lane < CROSS, value, 0)
    out = first
    for i in range(1, 4):
        out = out + pltpu.roll(first, CROSS * i, axis=1)
    return out


def starts(scalars, height):
    even = scalars[0] == 0
    start_a = pl.multiple_of(jnp.where(even, height, 0), 2 * PAD)
    start_b = pl.multiple_of(jnp.where(even, 0, height), 2 * PAD)
    return start_a, start_b


def sides(scalars, got_a, got_b):
    even = scalars[1] == 0
    from_a, from_b = got_a.astype(jnp.float32), got_b.astype(jnp.float32)
    return jnp.where(even, from_b, from_a), jnp.where(even, from_a, from_b)


def low_columns(from_left, b, lane):
    return jnp.where(lane < PAD, pltpu.roll(from_left, LANES - CROSS * b - PAD, axis=1), 0.0)


def high_columns(from_right, b, lane):
    return jnp.where(lane >= LANES - PAD, pltpu.roll(from_right, LANES - CROSS * b - PAD, axis=1), 0.0)


def edge_kernel(
    scalars, pos_hbm, amp_hbm, psf_rows_hbm, psf_cols_hbm, image_hbm,
    send_a, send_b, fine_y, fine_scaled, table_x, cross_fine_y, cross_fine_scaled, cross_x, tiles, amp, image,
    pos, psf_rows, psf_cols, sems, tmpl_y, tmpl_x, flux, fine_x, strips, cross_fine_x, cross_strips,
):
    comps, bands, taps = psf_rows.shape
    height, width = image.shape[1], image.shape[2]
    even = scalars[0] == 0
    copies = [
        pltpu.make_async_copy(pos_hbm, pos, sems.at[0]),
        pltpu.make_async_copy(psf_cols_hbm, psf_cols, sems.at[1]),
        pltpu.make_async_copy(psf_rows_hbm, psf_rows, sems.at[2]),
        pltpu.make_async_copy(amp_hbm, amp, sems.at[3]),
        pltpu.make_async_copy(image_hbm, image, sems.at[4]),
    ]
    for copy in copies:
        copy.start()
    live = scalars[2]
    lane = lax.broadcasted_iota(jnp.int32, (1, LANES), 1)
    base = (lane // CROSS) * CROSS
    tmpl_y[...] = jnp.zeros_like(tmpl_y)
    tmpl_x[...] = jnp.zeros_like(tmpl_x)
    cross_x[...] = jnp.zeros_like(cross_x)
    for copy in copies[:4]:
        copy.wait()
    tmpl_y[:, :, :taps] = psf_rows[...].astype(jnp.float32)
    tmpl_x[:, :, :taps] = psf_cols[...].astype(jnp.float32)
    flux[...] = jnp.where(lane < live, amp[...], 0.0)
    row, col = pos[0:1, :], pos[1:2, :]
    inner = lax.broadcasted_iota(jnp.int32, (3 * PAD, LANES), 0)

    def fine_index(centre, outside, add):
        tap = inner - (centre + 1) % PAD
        return jnp.where((tap >= 0) & (tap < taps), tap, outside) + add

    index_y, index_x = fine_index(row, LANES - 1, 0), fine_index(col, LANES - 1, 0)
    tile_y, tile_x = tiles_of(row), tiles_of(col)
    row_four, col_four = spread(row, lane), spread(col, lane)
    cross_index_y, cross_index_x = fine_index(row_four, CROSS - 1, base), fine_index(col_four, CROSS - 1, base)
    cross_tile_y, cross_tile_x = tiles_of(row_four), tiles_of(col_four)
    tiles[0] = tile_y
    tiles[1] = cross_tile_y

    four_y = grouped(tmpl_y[...])
    four_x = grouped(tmpl_x[...])
    four_flux = grouped(jnp.where(lane < CROSS, flux[...], 0.0))
    for b in range(bands):
        for j in range(comps // 4):
            cut = pl.ds((b * (comps // 4) + j) * LANES, LANES)
            placed = lookup(four_y[j][b : b + 1], cross_index_y)
            cross_fine_y[:, cut] = placed.astype(jnp.bfloat16)
            cross_fine_scaled[:, cut] = (placed * four_flux[j][b : b + 1]).astype(jnp.bfloat16)
            cross_fine_x[:, cut] = lookup(four_x[j][b : b + 1], cross_index_x).astype(jnp.bfloat16)
            for side_at, tile in ((0, 0), (PAD, width // PAD + 1)):
                value = jnp.zeros((PAD, LANES), jnp.bfloat16)
                for p in range(3):
                    value = jnp.where(cross_tile_x == tile - p, cross_fine_x[pl.ds(PAD * p, PAD), cut], value)
                cross_x[pl.ds(b * CROSS + side_at, PAD), cut] = value

    def edges(dst, src, tile, columns):
        place(dst, src, 0, 2, tile, 0, columns)
        place(dst, src, height // PAD, 2, tile, 2 * PAD, columns)

    edges(cross_strips, cross_fine_scaled, cross_tile_y, cross_strips.shape[1])
    wide = -lax.dot_general(cross_strips[...], cross_x[...], NT, preferred_element_type=jnp.float32)

    def fill(to, top, bottom, part):
        send_a[to, part] = jnp.where(even, bottom, top).astype(jnp.bfloat16)
        send_b[to, part] = jnp.where(even, top, bottom).astype(jnp.bfloat16)

    extra = pl.ds(bands * 2 * PAD, PAD)
    fill(extra, wide[:PAD], wide[2 * PAD : 3 * PAD], pl.ds(0, LANES))
    fill(extra, wide[PAD : 2 * PAD], wide[3 * PAD :], pl.ds(LANES, LANES))
    for b in range(bands):
        for k in range(comps):
            cut = pl.ds(k * LANES, LANES)
            placed = lookup(tmpl_y[k, b : b + 1, :], index_y)
            fine_y[b, :, cut] = placed.astype(jnp.bfloat16)
            fine_scaled[b, :, cut] = (placed * flux[k, b : b + 1, :]).astype(jnp.bfloat16)
            fine_x[b, :, cut] = lookup(tmpl_x[k, b : b + 1, :], index_x).astype(jnp.bfloat16)
        place(table_x.at[b], fine_x.at[b], 1, width // PAD, tile_x, 0, comps * LANES)
        edges(strips.at[b], fine_scaled.at[b], tile_y, comps * LANES)
        model = -lax.dot_general(strips[b], table_x[b], NT, preferred_element_type=jnp.float32)
        if b == 0:
            copies[4].wait()
        top_in = image[b, pl.ds(0, PAD), :].astype(jnp.float32)
        bottom_in = image[b, pl.ds(height - PAD, PAD), :].astype(jnp.float32)
        every = pl.ds(0, width)
        fill(pl.ds(b * 2 * PAD, PAD), model[:PAD], model[2 * PAD : 3 * PAD] + bottom_in, every)
        fill(pl.ds(b * 2 * PAD + PAD, PAD), model[PAD : 2 * PAD] + top_in, model[3 * PAD :], every)


def pack(low, high, wide, lane):
    to_left = to_right = wide
    for b in range(len(low)):
        shift = CROSS * b + PAD
        to_left = jnp.where((lane >= shift) & (lane < shift + PAD), pltpu.roll(low[b], shift, axis=1), to_left)
        to_right = jnp.where((lane >= shift - PAD) & (lane < shift), pltpu.roll(high[b], shift, axis=1), to_right)
    return to_left, to_right


def render_kernel(
    image, tiles, fine_scaled, table_x, cross_fine_scaled, cross_x,
    field, side, to_left, to_right, scaled, cross_scaled,
):
    bands, ext, width = field.shape
    height = ext - 2 * PAD
    lane = lax.broadcasted_iota(jnp.int32, (1, LANES), 1)
    place(cross_scaled, cross_fine_scaled, 0, ext // PAD, tiles[1], 0, cross_scaled.shape[1])
    side[...] = -lax.dot_general(cross_scaled[...], cross_x[...], NT, preferred_element_type=jnp.float32)
    for b in range(bands):
        place(scaled.at[b], fine_scaled.at[b], 0, ext // PAD, tiles[0], 0, scaled.shape[2])
        model = lax.dot_general(scaled[b], table_x[b], NT, preferred_element_type=jnp.float32)
        field[b, pl.ds(0, PAD), :] = -model[:PAD]
        field[b, pl.ds(PAD, height), :] = image[b].astype(jnp.float32) - model[PAD : PAD + height]
        field[b, pl.ds(PAD + height, PAD), :] = -model[PAD + height :]
    low = [field[b, :, pl.ds(0, LANES)] for b in range(bands)]
    high = [field[b, :, pl.ds(width - LANES, LANES)] for b in range(bands)]
    to_left[...], to_right[...] = pack(low, high, side[...], lane)


def column_kernel(scalars, left_in, right_in, got_b, got_a, send_a, send_b, to_left, to_right):
    ext = left_in.shape[0]
    lane = lax.broadcasted_iota(jnp.int32, (1, LANES), 1)
    to_left[...] = left_in[...]
    to_right[...] = right_in[...]
    bands = (got_a.shape[0] - PAD) // (2 * PAD)
    width = got_a.shape[1]
    for got, start in zip((got_a, got_b), starts(scalars, ext - 2 * PAD)):
        value = got[...].astype(jnp.float32)
        low = [value[b * 2 * PAD : (b + 1) * 2 * PAD, :LANES] for b in range(bands)]
        high = [value[b * 2 * PAD : (b + 1) * 2 * PAD, width - LANES :] for b in range(bands)]
        extra = value[bands * 2 * PAD :]
        wide = jnp.concatenate([extra[:, :LANES], extra[:, LANES : 2 * LANES]], axis=0)
        left, right = pack(low, high, wide, lane)
        to_left[pl.ds(start, 2 * PAD), :] += left
        to_right[pl.ds(start, 2 * PAD), :] += right
    even = scalars[1] == 0
    send_a[...] = jnp.where(even, to_right[...], to_left[...]).astype(jnp.bfloat16)
    send_b[...] = jnp.where(even, to_left[...], to_right[...]).astype(jnp.bfloat16)


def place_kernel(tiles, fine_y, cross_fine_y, ready, table_y, cross_y):
    bands, ext, columns = table_y.shape
    tile_y, cross_tile_y = tiles[0], tiles[1]

    def one_band(b, carry):
        place(table_y.at[b], fine_y.at[b], 0, ext // PAD, tile_y, 0, columns)
        return carry

    lax.fori_loop(0, bands, one_band, 0)
    place(cross_y, cross_fine_y, 0, ext // PAD, cross_tile_y, 0, cross_y.shape[1])


def gradient_kernel(
    scalars, amp, field, side, cols_b, cols_a, rows_b, rows_a, table_y, table_x, cross_y, cross_x,
    updated, residual, total, outer, gradient, sem,
):
    bands, ext, width = field.shape
    height = ext - 2 * PAD
    comps = amp.shape[0]
    live = scalars[2]
    lane = lax.broadcasted_iota(jnp.int32, (1, LANES), 1)
    from_left, from_right = sides(scalars, cols_a[...], cols_b[...])
    for b in range(bands):
        total[b, :, pl.ds(0, LANES)] = field[b, :, pl.ds(0, LANES)] + low_columns(from_left, b, lane)
        total[b, :, pl.ds(LANES, LANES)] = field[b, :, pl.ds(LANES, LANES)] + high_columns(from_right, b, lane)
    outer[...] = side[...] + jnp.where(lane % CROSS < PAD, from_left, from_right)
    for got, start in zip((rows_a, rows_b), starts(scalars, height)):
        for b in range(bands):
            total[b, pl.ds(start, 2 * PAD), :] += got[pl.ds(b * 2 * PAD, 2 * PAD), :].astype(jnp.float32)
        extra = pl.ds(bands * 2 * PAD, PAD)
        outer[pl.ds(start, PAD), :] += got[extra, pl.ds(0, LANES)].astype(jnp.float32)
        outer[pl.ds(start + PAD, PAD), :] += got[extra, pl.ds(LANES, LANES)].astype(jnp.float32)
    leaving = pltpu.make_async_copy(total.at[:, pl.ds(PAD, height), :], residual, sem)
    leaving.start()

    low_row, high_row, low_col, high_col = scalars[3], scalars[4], scalars[5], scalars[6]
    pixel_y = lax.broadcasted_iota(jnp.int32, (ext, LANES), 0)
    inside = (pixel_y >= low_row) & (pixel_y < high_row)
    inside = inside & (lane % CROSS >= low_col) & (lane % CROSS < high_col)
    beyond = jnp.where(inside, outer[...], 0.0).astype(jnp.bfloat16)

    total[:, pl.ds(0, PAD), :] = jnp.where(low_row > 0, 0.0, total[:, pl.ds(0, PAD), :])
    total[:, pl.ds(ext - PAD, PAD), :] = jnp.where(high_row < ext, 0.0, total[:, pl.ds(ext - PAD, PAD), :])
    for b in range(bands):
        rounded = total[b].astype(jnp.bfloat16)
        for k in range(0, comps, 2):
            cut = pl.ds(k * LANES, 2 * LANES)
            inner = lax.dot_general(rounded, table_x[b, :, cut], NN, preferred_element_type=jnp.float32)
            summed = jnp.sum(inner * table_y[b, :, cut].astype(jnp.float32), axis=0, keepdims=True)
            gradient[k, b : b + 1, :] = summed[:, :LANES]
            gradient[k + 1, b : b + 1, :] = summed[:, LANES:]

    inner = lax.dot_general(beyond, cross_x[...], NN, preferred_element_type=jnp.float32)
    summed = jnp.sum(inner * cross_y[...].astype(jnp.float32), axis=0, keepdims=True)
    for b in range(bands):
        for j in range(comps // 4):
            start = (b * (comps // 4) + j) * LANES
            four = summed[:, start : start + LANES]
            for i in range(4):
                part = four if i == 0 else pltpu.roll(four, LANES - CROSS * i, axis=1)
                gradient[4 * j + i, b : b + 1, :] += jnp.where(lane < CROSS, part, 0.0)
    updated[...] = amp[...] + step_rate * jnp.where(lane < live, gradient[...], 0.0)
    leaving.wait()


SMEM = pl.BlockSpec(memory_space=pltpu.SMEM)
VMEM = pl.BlockSpec(memory_space=pltpu.VMEM)
HBM = pl.BlockSpec(memory_space=pltpu.HBM)
params = pltpu.CompilerParams(vmem_limit_bytes=16 << 20)


def swaps(axis, first):
    out = []
    for i in range(first, lax.axis_size(axis) - 1, 2):
        out += [(i, i + 1), (i + 1, i)]
    return out


def on_device(image, amplitude, positions, live, psf_rows, psf_cols):
    amp = jnp.swapaxes(amplitude[0, 0], 0, 1)
    psf_rows, psf_cols = jnp.swapaxes(psf_rows, 0, 1), jnp.swapaxes(psf_cols, 0, 1)
    bands, height, width = image.shape
    comps, slots = amp.shape[0], amp.shape[2]
    ext = height + 2 * PAD
    shape = jax.ShapeDtypeStruct
    f32, bf16 = jnp.float32, jnp.bfloat16
    region, tile = lax.axis_index("region"), lax.axis_index("tile")
    scalars = jnp.stack([
        region % 2,
        tile % 2,
        live[0, 0],
        jnp.where(region == 0, PAD, 0),
        jnp.where(region == lax.axis_size("region") - 1, ext - PAD, ext),
        jnp.where(tile == 0, PAD, 0),
        jnp.where(tile == lax.axis_size("tile") - 1, PAD, 2 * PAD),
    ]).astype(jnp.int32)
    rows_sent = bands * 2 * PAD + PAD
    table_width = comps * slots
    cross_width = bands * comps * CROSS
    centres = positions[:, 0, 0]
    strip = shape((ext, LANES), bf16)
    fine = shape((bands, 3 * PAD, table_width), bf16)
    cross_fine = shape((3 * PAD, cross_width), bf16)
    (
        send_a, send_b, fine_y, fine_scaled, table_x, cross_fine_y, cross_fine_scaled, cross_x, tiles, amp, image,
    ) = pl.pallas_call(
        edge_kernel,
        out_shape=[
            shape((rows_sent, width), bf16), shape((rows_sent, width), bf16),
            fine, fine, shape((bands, width, table_width), bf16),
            cross_fine, cross_fine, shape((bands * CROSS, cross_width), bf16),
            shape((2, PAD, LANES), bf16), shape(amp.shape, f32), shape(image.shape, bf16),
        ],
        in_specs=[SMEM] + [HBM] * 5,
        out_specs=[VMEM] * 11,
        scratch_shapes=[
            pltpu.VMEM(centres.shape, jnp.int32),
            pltpu.VMEM(psf_rows.shape, bf16), pltpu.VMEM(psf_cols.shape, bf16), pltpu.SemaphoreType.DMA((5,)),
            pltpu.VMEM((comps, bands, LANES), f32), pltpu.VMEM((comps, bands, LANES), f32),
            pltpu.VMEM((comps, bands, LANES), f32), pltpu.VMEM((bands, 3 * PAD, table_width), bf16),
            pltpu.VMEM((bands, 4 * PAD, table_width), bf16), pltpu.VMEM((3 * PAD, cross_width), bf16),
            pltpu.VMEM((4 * PAD, cross_width), bf16),
        ],
        compiler_params=params,
    )(scalars, *[pltpu.with_memory_space_constraint(x, pltpu.HBM) for x in (centres, amp, psf_rows, psf_cols, image)])
    rows_b = lax.ppermute(send_b, "region", swaps("region", 1))
    rows_a = lax.ppermute(send_a, "region", swaps("region", 0))
    field, side, to_left, to_right = pl.pallas_call(
        render_kernel,
        out_shape=[
            shape((bands, ext, width), f32), shape((ext, LANES), f32),
            shape((ext, LANES), f32), shape((ext, LANES), f32),
        ],
        in_specs=[VMEM] * 6,
        out_specs=[VMEM] * 4,
        scratch_shapes=[pltpu.VMEM((bands, ext, table_width), bf16), pltpu.VMEM((ext, cross_width), bf16)],
        compiler_params=params,
    )(image, tiles, fine_scaled, table_x, cross_fine_scaled, cross_x)
    send_a, send_b = pl.pallas_call(
        column_kernel,
        out_shape=[strip, strip],
        in_specs=[SMEM] + [VMEM] * 4,
        out_specs=[VMEM] * 2,
        scratch_shapes=[pltpu.VMEM((ext, LANES), f32), pltpu.VMEM((ext, LANES), f32)],
        compiler_params=params,
    )(scalars, to_left, to_right, rows_b, rows_a)
    cols_b = lax.ppermute(send_b, "tile", swaps("tile", 1))
    cols_a = lax.ppermute(send_a, "tile", swaps("tile", 0))
    table_y, cross_y = pl.pallas_call(
        place_kernel,
        out_shape=[shape((bands, ext, table_width), bf16), shape((ext, cross_width), bf16)],
        in_specs=[VMEM] * 4,
        out_specs=[VMEM] * 2,
        compiler_params=params,
    )(tiles, fine_y, cross_fine_y, send_a)
    updated, residual = pl.pallas_call(
        gradient_kernel,
        out_shape=[shape(amp.shape, f32), shape(image.shape, f32)],
        in_specs=[SMEM] + [VMEM] * 11,
        out_specs=[VMEM, HBM],
        scratch_shapes=[
            pltpu.VMEM((bands, ext, width), f32), pltpu.VMEM((ext, LANES), f32),
            pltpu.VMEM((comps, bands, LANES), f32), pltpu.SemaphoreType.DMA,
        ],
        compiler_params=params,
    )(scalars, amp, field, side, cols_b, cols_a, rows_b, rows_a, table_y, table_x, cross_y, cross_x)
    return (jnp.swapaxes(updated, 0, 1)[None, None], residual)


def solution(mesh):
    in_specs = (
        P(None, "region", "tile"),
        P("region", "tile", None, None, None),
        P(None, "region", "tile", None),
        P("region", "tile"),
        P(),
        P(),
    )
    out_specs = (P("region", "tile", None, None, None), P(None, "region", "tile"))
    return jax.shard_map(
        on_device, mesh=mesh, in_specs=in_specs, out_specs=out_specs, check_vma=False
    )
```
